32 devices in a mesh: sweep: 16 (over z, y, x), cols: 2 (over core).
Axes of the slice: x: 2, y: 2, z: 4, core: 2. Of those that a mesh axis runs over, the one named last changes fastest.
Arguments:
- rhs: bfloat16 [4, 16, 256, 1024], P(None, 'sweep', None, 'cols'), may hold values from -6 to 6
- blocks: bfloat16 [3, 16, 6, 256, 256], P(None, 'sweep', None, 'cols'), may hold values from -0.1875 to 0.1875
- diag_inv: bfloat16 [4, 16, 256, 256], P(None, 'sweep', 'cols'), as said below
- neighbours: int32 [3, 16, 6], P(None, 'sweep'), may hold values from -1 to 47, as said below
Outputs:
- samples: bfloat16 [4, 16, 256, 1024], P(None, 'sweep', None, 'cols')
The draws below stay inside these ranges and needn't reach their ends.
Inputs may be any that keep to these rules, and one draw needn't show every extreme that they name: neighbours[b, p, k] belongs to block row (b + 1, p): -1 marks an unused slot; a used slot names block row b * 16 + p - o for some o with 0 <= o <= min(5, p), and the used slots of one block row name distinct rows. The last owner's block rows use all 6 slots. `diag_inv`: every block is lower triangular with a positive diagonal.
All inputs are finite; a program needn't handle non-finite values.
Results may differ from the reference program's by a relative error of at most 0.0095.
Values may be sent and summed in bfloat16 or wider, within the bound.
A program may use at most 64 MiB of HBM per device.

```python
import math
import jax
import jax.numpy as jnp
from jax import lax

BS = 256
LEVELS = 4
KMAX = 6
REACH = 5
OWNERS = 16
NCOL = 1024


def draw_neighbours(key, part):
    key_perm, key_cap, key_count = jax.random.split(jax.random.fold_in(key, 11), 3)
    total_rows = (LEVELS - 1) * OWNERS
    row_keys = jax.random.split(key_perm, total_rows)
    perms = jax.vmap(lambda row_key: jax.random.permutation(row_key, REACH + 1))(row_keys)
    perms = perms[:, :KMAX].reshape(LEVELS - 1, OWNERS, KMAX).astype(jnp.int32)
    caps = jax.random.randint(key_cap, (OWNERS,), 1, KMAX + 1)
    counts = jax.random.randint(key_count, (LEVELS - 1, OWNERS), 1, caps[None, :] + 1)
    owner = jnp.arange(OWNERS, dtype=jnp.int32)[None, :]
    counts = jnp.where(owner == OWNERS - 1, KMAX, counts)
    slot = jnp.arange(KMAX, dtype=jnp.int32)[None, None, :]
    level = jnp.arange(LEVELS - 1, dtype=jnp.int32)[:, None, None]
    used = (slot < counts[:, :, None]) & (perms <= owner[:, :, None])
    return jnp.where(used, level * OWNERS + owner[:, :, None] - perms, -1).astype(jnp.int32)


def draw_diag_inv(key, part):
    key_off, key_diag = jax.random.split(jax.random.fold_in(key, 23))
    shape = (LEVELS, OWNERS, BS, BS)
    offdiag = jax.random.normal(key_off, shape, jnp.float32) / math.sqrt(BS)
    diagonal = jnp.exp(jax.random.uniform(key_diag, (LEVELS, OWNERS, BS), jnp.float32, math.log(0.5), math.log(2.0)))
    rows = jnp.arange(BS)[:, None]
    cols = jnp.arange(BS)[None, :]
    lower = jnp.where(rows > cols, offdiag, 0.0)
    eye = (rows == cols).astype(jnp.float32)
    return (lower + diagonal[..., None] * eye).astype(jnp.bfloat16)


def steps_of(key, shape, shards, smallest, largest):
    loudness, own = 1.0, jax.random.fold_in(key, 6)
    for dim, blocks in shards:
        heights = jnp.exp(jax.random.uniform(jax.random.fold_in(own, dim), (blocks,), jnp.float32, smallest / len(shards), largest / len(shards)))
        loudness = loudness * jnp.repeat(heights, shape[dim] // blocks).reshape([-1 if axis == dim else 1 for axis in range(len(shape))])
    return loudness


def gaussian(key, dims, scale, reach, cuts=(), kind=jnp.bfloat16):
    loudness = steps_of(key, dims, cuts, -0.22, 0.18) if cuts else 1.0
    result = jax.random.normal(key, dims, jnp.float32) * scale * loudness
    return jnp.minimum(jnp.maximum(result, -reach), reach).astype(kind)


def setup_inputs(seed: int = 0) -> dict:
    keys = jax.random.split(jax.random.key(seed), 5)
    return {
        "rhs": gaussian(keys[0], (LEVELS, OWNERS, BS, NCOL), 1.0, 6.0, ((1, 16), (3, 2))),
        "blocks": gaussian(keys[1], (LEVELS - 1, OWNERS, KMAX, BS, BS), (4 * BS) ** -0.5, 0.1875, ((1, 16), (3, 2))),
        "diag_inv": draw_diag_inv(jax.random.fold_in(keys[4], 71), 0),
        "neighbours": draw_neighbours(jax.random.fold_in(keys[4], 71), 0),
    }


def reference(rhs, blocks, diag_inv, neighbours):
    owners = rhs.shape[1]
    solved = [jnp.einsum('pab,pbc->pac', diag_inv[0].astype(jnp.float32), rhs[0].astype(jnp.float32)).astype(jnp.bfloat16)]
    for level in range(1, LEVELS):
        row_ids = neighbours[level - 1]
        valid = (row_ids >= 0).astype(jnp.float32)
        local = jnp.clip(row_ids - (level - 1) * owners, 0, owners - 1).astype(jnp.int32)
        sums = jnp.zeros(rhs.shape[1:], jnp.float32)
        for slot in range(KMAX):
            picked = solved[level - 1][local[:, slot]].astype(jnp.float32) * valid[:, slot][:, None, None]
            sums = sums + jnp.einsum('pab,pbc->pac', blocks[level - 1, :, slot].astype(jnp.float32), picked)
        residue = (rhs[level].astype(jnp.float32) - sums).astype(jnp.bfloat16)
        solved.append(jnp.einsum('pab,pbc->pac', diag_inv[level].astype(jnp.float32), residue.astype(jnp.float32)).astype(jnp.bfloat16))
    top = LEVELS - 1
    samples = [None] * LEVELS
    samples[top] = jnp.einsum('pba,pbc->pac', diag_inv[top].astype(jnp.float32), solved[top].astype(jnp.float32)).astype(jnp.bfloat16)
    for level in range(LEVELS - 2, -1, -1):
        row_ids = neighbours[level]
        valid = (row_ids >= 0).astype(jnp.float32)
        local = jnp.clip(row_ids - level * owners, 0, owners - 1).astype(jnp.int32)
        upper = samples[level + 1].astype(jnp.float32)
        back_terms = jnp.zeros(rhs.shape[1:], jnp.float32)
        for slot in range(KMAX):
            term = jnp.einsum('pba,pbc->pac', blocks[level, :, slot].astype(jnp.float32), upper) * valid[:, slot][:, None, None]
            term = lax.optimization_barrier(term.astype(jnp.bfloat16)).astype(jnp.float32)
            back_terms = back_terms.at[local[:, slot]].add(term)
        adjusted = (solved[level].astype(jnp.float32) - back_terms).astype(jnp.bfloat16)
        samples[level] = jnp.einsum('pba,pbc->pac', diag_inv[level].astype(jnp.float32), adjusted.astype(jnp.float32)).astype(jnp.bfloat16)
    return jnp.stack(samples)
```

```python
import functools

import jax
import jax.numpy as jnp
from jax import lax
from jax.experimental import pallas as pl
from jax.experimental.pallas import tpu as pltpu
from jax.sharding import PartitionSpec as P

REACH = 5
GROUP = 4
F32 = jnp.float32
BF16 = jnp.bfloat16


def mm(a, b):
    return jnp.dot(a, b, preferred_element_type=F32)


def kernel(
    owners, ncores, nbr, rhs, blocks, diag, out,
    fac, raw, win, rloc, solved_t, samp_t, near, far, stage, ostage,
    s_own, r_own, s_dg, r_dg, s_core, r_core, s_rhs, r_rhs, s_loc,
    s_x, r_x, s_b, r_b, s_o, r_o, s_raw, s_diag,
):
    levels = rhs.shape[0]
    rows = diag.shape[2]
    slots = blocks.shape[2]
    width = rhs.shape[3] // GROUP
    planes = owners // GROUP
    me = lax.axis_index("sweep")
    c = lax.axis_index("cols")
    k = me // GROUP
    i = me % GROUP
    px = i + 1 - 2 * (i % 2)
    py = (i + 2) % GROUP
    dg = GROUP - 1 - i
    base = k * GROUP
    peers = (px, py, dg)

    def at(owner, core):
        return (owner, core)

    def remote(src, dst, ssem, rsem, dev):
        return pltpu.make_async_remote_copy(
            src_ref=src, dst_ref=dst, send_sem=ssem, recv_sem=rsem,
            device_id=dev, device_id_type=pl.DeviceIdType.MESH,
        )

    barrier = pltpu.get_barrier_semaphore()

    def greet(owner, core):
        pl.semaphore_signal(
            barrier, inc=1, device_id=at(owner, core), device_id_type=pl.DeviceIdType.MESH
        )

    for q in peers:
        greet(base + q, c)
    for r in range(1, ncores):
        greet(me, (c + r) % ncores)
    count = 3 + ncores - 1
    for d in (1, 2):
        @pl.when(k >= d)
        def _():
            greet(me - d * GROUP, c)

        @pl.when(k + d < planes)
        def _():
            greet(me + d * GROUP, c)

        count = count + jnp.where(k >= d, 1, 0) + jnp.where(k + d < planes, 1, 0)

    mine = pl.ds(pl.multiple_of(c * rows, rows), rows)

    def diag_local(t):
        return pltpu.make_async_copy(diag.at[t, 0], fac.at[t, i, REACH + 1, mine, :], s_diag.at[t])

    raw_local = pltpu.make_async_copy(blocks.at[:, 0], raw, s_raw)
    for t in range(levels):
        diag_local(t).start()
    raw_local.start()

    def clear(ref):
        ref[...] = jnp.zeros_like(ref)

    @pl.when(k == 0)
    def _():
        for l in range(levels - 1):
            clear(win.at[l, 0:REACH])

    @pl.when(k == 1)
    def _():
        for l in range(levels - 1):
            clear(win.at[l, 0])

    @pl.when(k + 1 >= planes)
    def _():
        clear(near)

    @pl.when((k + 1 >= planes) | (k < 1))
    def _():
        clear(far)

    def stage_level(t):
        diag_local(t).wait()
        if t == 0:
            return
        if t == 1:
            raw_local.wait()
        for o in range(REACH + 1):
            slot, hit = jnp.int32(0), jnp.int32(0)
            for s in range(slots):
                got = nbr[t - 1, 0, s]
                same = (got == (t - 1) * owners + me - o) & (got >= 0)
                slot = jnp.where(same, s, slot)
                hit = jnp.where(same, 1, hit)
            block = raw[t - 1, slot].astype(F32) * hit.astype(F32)
            fac[t, i, o, mine, :] = block.astype(BF16)

    pl.semaphore_wait(barrier, count)

    half = rows // 2

    def shard(t, owner):
        first = REACH + 1 if t == 0 else 0
        return fac.at[t, owner, pl.ds(first, REACH + 2 - first), mine, :]

    def shard_half(t, owner, h):
        first = REACH + 1 if t == 0 else 0
        part = pl.ds(pl.multiple_of(c * rows + h * half, half), half)
        return fac.at[t, owner, pl.ds(first, REACH + 2 - first), part, :]

    def own_copy(t, n):
        ref = shard(t, i)
        return remote(ref, ref, s_own.at[t, n], r_own.at[t, n], at(base + peers[n], c))

    def diag_copy(t, n):
        ref = shard_half(t, peers[n], n)
        return remote(ref, ref, s_dg.at[t, n], r_dg.at[t, n], at(base + peers[1 - n], c))

    def core_copy(t, source, r):
        ref = shard(t, ((i,) + peers)[source])
        return remote(
            ref, ref, s_core.at[t, source, r - 1], r_core.at[t, source, r - 1],
            at(me, (c + r) % ncores),
        )

    def rhs_copy(t, n):
        q = peers[n]
        cols = pl.ds(pl.multiple_of(q * width, width), width)
        return remote(
            rhs.at[t, 0, :, cols], rloc.at[t, i], s_rhs.at[t, n], r_rhs.at[t, n], at(base + q, c)
        )

    def rhs_local(t):
        cols = pl.ds(pl.multiple_of(i * width, width), width)
        return pltpu.make_async_copy(rhs.at[t, 0, :, cols], rloc.at[t, i], s_loc.at[t])

    cores = range(1, ncores)

    def start(t):
        for n in range(3):
            rhs_copy(t, n).start()
        rhs_local(t).start()
        stage_level(t)
        for n in range(2):
            own_copy(t, n).start()
        for r in cores:
            core_copy(t, 0, r).start()

    def forward(t):
        for n in range(2):
            own_copy(t, n).wait_recv()
            diag_copy(t, n).start()
            for r in cores:
                core_copy(t, 1 + n, r).start()

    def finish_diag(t):
        for n in range(2):
            diag_copy(t, n).wait_recv()
        for r in cores:
            core_copy(t, 3, r).start()

    def arrived(t):
        for n in range(3):
            rhs_copy(t, n).wait_recv()
        rhs_local(t).wait()
        for source in range(4):
            for r in cores:
                core_copy(t, source, r).wait_recv()

    def sent(t):
        for n in range(3):
            rhs_copy(t, n).wait_send()
        for n in range(2):
            own_copy(t, n).wait_send()
            diag_copy(t, n).wait_send()
        for source in range(4):
            for r in cores:
                core_copy(t, source, r).wait_send()

    def solved_copy(l, n):
        j = GROUP - 1 if n == GROUP else n
        step, spot = (2, 0) if n == GROUP else (1, 1 + n)
        return remote(
            win.at[l, REACH + j], win.at[l, spot], s_x.at[l, n], r_x.at[l, n],
            at(me + step * GROUP, c),
        )

    def solve(l):
        for j in (range(GROUP) if l == levels - 1 else reversed(range(GROUP))):
            res = rloc[l, j]
            if l > 0:
                acc = mm(fac[l, j, 0], win[l - 1, REACH + j])
                for o in range(1, REACH + 1):
                    acc = acc + mm(fac[l, j, o], win[l - 1, REACH + j - o])
                res = (res.astype(F32) - acc).astype(BF16)
            y = mm(fac[l, j, REACH + 1], res)
            if l < levels - 1:
                win[l, REACH + j] = y.astype(BF16)

                @pl.when(k + 1 < planes)
                def _():
                    solved_copy(l, j).start()

                if j == GROUP - 1:
                    @pl.when(k + 2 < planes)
                    def _():
                        solved_copy(l, GROUP).start()

            solved_t[l, j] = y.T.astype(BF16)

    def solved_recv(l):
        @pl.when(k >= 1)
        def _():
            for n in range(GROUP):
                solved_copy(l, n).wait_recv()

        @pl.when(k >= 2)
        def _():
            solved_copy(l, GROUP).wait_recv()

    start(0)
    start(1)
    forward(0)
    if levels > 2:
        start(2)
    finish_diag(0)
    for l in range(levels):
        if l + 1 < levels:
            forward(l + 1)
        if l + 3 < levels:
            start(l + 3)
        arrived(l)
        if l > 0:
            solved_recv(l - 1)
        solve(l)
        if l + 1 < levels:
            finish_diag(l + 1)

    def term_copy(l, n):
        dst = far.at[l] if n == 0 else near.at[l, n - 1]
        return remote(stage.at[l, n], dst, s_b.at[l, n], r_b.at[l, n], at(me - GROUP, c))

    def out_cols(q):
        return pl.ds(pl.multiple_of(q * width, width), width)

    def out_copy(l, n, q):
        return remote(
            ostage.at[l, q], out.at[l, 0, :, out_cols(i)], s_o.at[l, n], r_o.at[l, n], at(base + q, c)
        )

    def out_local(l):
        return pltpu.make_async_copy(ostage.at[l, i], out.at[l, 0, :, out_cols(i)], s_o.at[l, 3])

    def emit(l, j):
        ostage[l, j] = samp_t[l, j].astype(F32).T.astype(BF16)
        jx, jy = j % 2, j // 2
        ix, iy = i % 2, i // 2
        n = 2 * (iy + jy - 2 * iy * jy) + (ix + jx - 2 * ix * jx) - 1

        @pl.when(i == j)
        def _():
            out_local(l).start()

        @pl.when(i != j)
        def _():
            out_copy(l, n, j).start()

    def terms(l, w):
        total = None
        for j in range(max(0, w - REACH), min(GROUP - 1, w) + 1):
            term = mm(samp_t[l + 1, j], fac[l + 1, j, REACH + j - w])
            total = term if total is None else total + term
        return total

    def ship(l, w):
        total = terms(l, w)
        if w == REACH - 1:
            @pl.when((k + 1 < planes) & (k >= 1))
            def _():
                term_copy(l, 0).wait_recv()

            total = total + far[l].astype(F32)
        stage[l, w] = total.astype(BF16)

        @pl.when(k >= (2 if w == 0 else 1))
        def _():
            term_copy(l, w).start()

    top = levels - 1
    back = None
    for l in range(top, -1, -1):
        for j in range(GROUP):
            adjusted = solved_t[l, j]
            if l < top:
                @pl.when(k + 1 < planes)
                def _():
                    term_copy(l, j + 1).wait_recv()

                total = back[j] + near[l, j].astype(F32)
                adjusted = (adjusted.astype(F32) - total).astype(BF16)
            samp_t[l, j] = mm(adjusted, fac[l, j, REACH + 1]).astype(BF16)
            if l > 0:
                for w in range(REACH):
                    if min(GROUP - 1, w) == j:
                        ship(l - 1, w)
            emit(l, j)
        if l > 0:
            back = [terms(l - 1, REACH + j) for j in range(GROUP)]

    for t in range(levels):
        sent(t)
    for l in range(levels - 1):
        @pl.when(k + 1 < planes)
        def _():
            for n in range(GROUP):
                solved_copy(l, n).wait_send()

        @pl.when(k + 2 < planes)
        def _():
            solved_copy(l, GROUP).wait_send()

        @pl.when(k >= 1)
        def _():
            for n in range(1, REACH):
                term_copy(l, n).wait_send()

        @pl.when(k >= 2)
        def _():
            term_copy(l, 0).wait_send()

    for l in range(levels):
        for n in range(3):
            out_copy(l, n, peers[n]).wait()
        out_local(l).wait()


def on_device(rhs, blocks, diag_inv, neighbours):
    owners = lax.axis_size("sweep")
    ncores = lax.axis_size("cols")
    levels, _, bs, cols = rhs.shape
    width = cols // GROUP
    dma = pltpu.SemaphoreType.DMA
    hbm = pl.BlockSpec(memory_space=pltpu.HBM)
    return pl.pallas_call(
        functools.partial(kernel, owners, ncores),
        out_shape=jax.ShapeDtypeStruct(rhs.shape, rhs.dtype),
        in_specs=[pl.BlockSpec(memory_space=pltpu.SMEM), hbm, hbm, hbm],
        out_specs=hbm,
        scratch_shapes=[
            pltpu.VMEM((levels, GROUP, REACH + 2, bs, bs), BF16),
            pltpu.VMEM(blocks.shape[:1] + blocks.shape[2:], BF16),
            pltpu.VMEM((levels - 1, REACH + GROUP, bs, width), BF16),
            pltpu.VMEM((levels, GROUP, bs, width), BF16),
            pltpu.VMEM((levels, GROUP, width, bs), BF16),
            pltpu.VMEM((levels, GROUP, width, bs), BF16),
            pltpu.VMEM((levels - 1, GROUP, width, bs), BF16),
            pltpu.VMEM((levels - 1, width, bs), BF16),
            pltpu.VMEM((levels - 1, REACH, width, bs), BF16),
            pltpu.VMEM((levels, GROUP, bs, width), BF16),
            dma((levels, 2)), dma((levels, 2)),
            dma((levels, 2)), dma((levels, 2)),
            dma((levels, 4, ncores - 1)), dma((levels, 4, ncores - 1)),
            dma((levels, 3)), dma((levels, 3)), dma((levels,)),
            dma((levels - 1, REACH)), dma((levels - 1, REACH)),
            dma((levels - 1, REACH)), dma((levels - 1, REACH)),
            dma((levels, 4)), dma((levels, 3)), dma, dma((levels,)),
        ],
        compiler_params=pltpu.CompilerParams(
            collective_id=0, has_side_effects=True, vmem_limit_bytes=62 << 20
        ),
    )(neighbours, rhs, blocks, diag_inv)


def solution(mesh):
    placed = (
        P(None, "sweep", None, "cols"),
        P(None, "sweep", None, "cols", None),
        P(None, "sweep", "cols", None),
        P(None, "sweep", None),
    )
    return jax.shard_map(
        on_device,
        mesh=mesh,
        in_specs=placed,
        out_specs=P(None, "sweep", None, "cols"),
        check_vma=False,
    )
```

```python
import functools

import jax
import jax.numpy as jnp
from jax import lax
from jax.experimental import pallas as pl
from jax.experimental.pallas import tpu as pltpu
from jax.sharding import PartitionSpec as P

REACH = 5
GROUP = 4
F32 = jnp.float32
BF16 = jnp.bfloat16

SLOT = {0: 0, 4: 1, 1: 2, 2: 3, 3: 4, 5: 5}
DIAG = REACH + 1


def parts_of(levels):
    early = [(1, 2, 2), (1, 4, 3)]
    for t in range(2, levels):
        early += [(t, 0, 4), (t, 4, 3)]
    return early + [(1, 0, 2), (0, DIAG, 1)], len(early)


def mm(a, b):
    return jnp.dot(a, b, preferred_element_type=F32)


def kernel(
    owners, ncores, nbr, rhs, blocks, diag, out,
    fac, raw, wide, first, below, shifted, win, rloc, solved_t, samp_t, near, far, stage, ostage,
    s_own, r_own, s_dg, r_dg, s_core, r_core, s_rhs, r_rhs, s_loc,
    s_up, r_up, s_x, r_x, s_b, r_b, s_o, r_o, s_raw, s_diag, s_wide,
):
    levels = rhs.shape[0]
    rows = diag.shape[2]
    slots = blocks.shape[2]
    width = rhs.shape[3] // GROUP
    planes = owners // GROUP
    top = levels - 1
    parts, n_early = parts_of(levels)
    me = lax.axis_index("sweep")
    c = lax.axis_index("cols")
    k = me // GROUP
    i = me % GROUP
    px = i + 1 - 2 * (i % 2)
    py = (i + 2) % GROUP
    dg = GROUP - 1 - i
    base = k * GROUP
    peers = (px, py, dg)
    sources = (i,) + peers
    cores = range(1, ncores)

    def at(owner, core):
        return (owner, core)

    def remote(src, dst, ssem, rsem, dev):
        return pltpu.make_async_remote_copy(
            src_ref=src, dst_ref=dst, send_sem=ssem, recv_sem=rsem,
            device_id=dev, device_id_type=pl.DeviceIdType.MESH,
        )

    barrier = pltpu.get_barrier_semaphore()

    def greet(owner, core):
        pl.semaphore_signal(
            barrier, inc=1, device_id=at(owner, core), device_id_type=pl.DeviceIdType.MESH
        )

    for q in peers:
        greet(base + q, c)
    for r in range(1, ncores):
        greet(me, (c + r) % ncores)
    count = 3 + ncores - 1
    for d in (1, 2):
        @pl.when(k >= d)
        def _():
            greet(me - d * GROUP, c)

        @pl.when(k + d < planes)
        def _():
            greet(me + d * GROUP, c)

        count = count + jnp.where(k >= d, 1, 0) + jnp.where(k + d < planes, 1, 0)

    mine = pl.ds(pl.multiple_of(c * rows, rows), rows)

    def diag_local(t):
        return pltpu.make_async_copy(diag.at[t, 0], fac.at[t, i, DIAG, mine, :], s_diag.at[t])

    def wide_local(t):
        return pltpu.make_async_copy(rhs.at[t, 0], wide.at[t], s_wide.at[t])

    raw_local = pltpu.make_async_copy(blocks.at[:, 0], raw, s_raw)
    diag_local(0).start()
    raw_local.start()
    for t in range(2):
        wide_local(t).start()
    for t in range(1, levels):
        diag_local(t).start()

    def clear(ref):
        ref[...] = jnp.zeros_like(ref)

    @pl.when(k == 0)
    def _():
        clear(below)
        for l in range(levels - 1):
            clear(win.at[l, 0:REACH])

    @pl.when(k == 1)
    def _():
        for l in range(levels - 1):
            clear(win.at[l, 0])

    @pl.when(k + 1 >= planes)
    def _():
        clear(near)

    @pl.when((k + 1 >= planes) | (k < 1))
    def _():
        clear(far)

    def stage_level(t):
        for o in range(REACH + 1):
            slot, hit = jnp.int32(0), jnp.int32(0)
            for s in range(slots):
                got = nbr[t - 1, 0, s]
                same = (got == (t - 1) * owners + me - o) & (got >= 0)
                slot = jnp.where(same, s, slot)
                hit = jnp.where(same, 1, hit)
            block = raw[t - 1, slot].astype(F32) * hit.astype(F32)
            fac[t, i, SLOT[o], mine, :] = block.astype(BF16)
        diag_local(t).wait()

    half = rows // 2

    def shard(p, owner):
        t, lo, n = parts[p]
        return fac.at[t, owner, pl.ds(lo, n), mine, :]

    def shard_half(p, owner, h):
        t, lo, n = parts[p]
        part = pl.ds(pl.multiple_of(c * rows + h * half, half), half)
        return fac.at[t, owner, pl.ds(lo, n), part, :]

    def own_copy(p, n):
        ref = shard(p, i)
        return remote(ref, ref, s_own.at[p, n], r_own.at[p, n], at(base + peers[n], c))

    def diag_copy(p, n):
        ref = shard_half(p, peers[n], n)
        return remote(ref, ref, s_dg.at[p, n], r_dg.at[p, n], at(base + peers[1 - n], c))

    def core_copy(p, source, r):
        ref = shard(p, sources[source])
        return remote(
            ref, ref, s_core.at[p, source, r - 1], r_core.at[p, source, r - 1],
            at(me, (c + r) % ncores),
        )

    def columns(q):
        return pl.ds(pl.multiple_of(q * width, width), width)

    def deal(t, q):
        if t == 0:
            return first.at[:, columns(q)], win.at[0, REACH + i]
        if t == 1:
            return shifted.at[:, columns(q)], rloc.at[1, i]
        return rhs.at[t, 0, :, columns(q)], rloc.at[t, i]

    def deal_copy(t, n):
        src, dst = deal(t, peers[n])
        return remote(src, dst, s_rhs.at[t, n], r_rhs.at[t, n], at(base + peers[n], c))

    def deal_local(t):
        src, dst = deal(t, i)
        return pltpu.make_async_copy(src, dst, s_loc.at[t])

    def deal_start(t):
        for n in range(3):
            deal_copy(t, n).start()
        deal_local(t).start()

    def deal_wait(t):
        for n in range(3):
            deal_copy(t, n).wait_recv()
        deal_local(t).wait()

    def core_start(p, source):
        for r in cores:
            core_copy(p, source, r).start()

    def core_wait(p, source):
        for r in cores:
            core_copy(p, source, r).wait_recv()

    def start(p):
        for n in range(2):
            own_copy(p, n).start()

    def forward(p):
        for n in range(2):
            own_copy(p, n).wait_recv()
            diag_copy(p, n).start()
            core_start(p, 1 + n)

    def finish_diag(p):
        for n in range(2):
            diag_copy(p, n).wait_recv()
        core_start(p, 3)

    def up_copy():
        return remote(first, below, s_up, r_up, at(me + GROUP, c))

    def solved_copy(l, n):
        j = GROUP - 1 if n == GROUP else n
        step, spot = (2, 0) if n == GROUP else (1, 1 + n)
        return remote(
            win.at[l, REACH + j], win.at[l, spot], s_x.at[l, n], r_x.at[l, n],
            at(me + step * GROUP, c),
        )

    def solved_send(l, j):
        @pl.when(k + 1 < planes)
        def _():
            solved_copy(l, j).start()

        if j == GROUP - 1:
            @pl.when(k + 2 < planes)
            def _():
                solved_copy(l, GROUP).start()

    def solved_recv(l):
        @pl.when(k >= 1)
        def _():
            for n in range(GROUP):
                solved_copy(l, n).wait_recv()

        @pl.when(k >= 2)
        def _():
            solved_copy(l, GROUP).wait_recv()

    def solve(l, j):
        acc = None
        for o in range(REACH + 1):
            if l == 1 and SLOT[o] < 2:
                continue
            term = mm(fac[l, j, SLOT[o]], win[l - 1, REACH + j - o])
            acc = term if acc is None else acc + term
        res = (rloc[l, j].astype(F32) - acc).astype(BF16)
        return mm(fac[l, j, DIAG], res)

    def solve_level(l):
        for j in reversed(range(GROUP)):
            y = solve(l, j)
            win[l, REACH + j] = y.astype(BF16)
            solved_send(l, j)
            solved_t[l, j] = y.T.astype(BF16)

    late = (n_early, n_early + 1)
    raw_local.wait()
    stage_level(1)
    diag_local(0).wait()
    pl.semaphore_wait(barrier, count)

    core_start(late[1], 0)
    core_start(late[0], 0)
    for p in range(2):
        start(p)
        core_start(p, 0)
    wide_local(0).wait()
    core_wait(late[1], 0)
    first[...] = mm(fac[0, i, DIAG], wide[0]).astype(BF16)
    deal_start(0)

    @pl.when(k + 1 < planes)
    def _():
        up_copy().start()

    def begin(t):
        stage_level(t)
        deal_start(t)
        for p in range(2 * t - 2, 2 * t):
            start(p)
            core_start(p, 0)

    begin(2)
    forward(0)
    deal_wait(0)
    for j in reversed(range(GROUP)):
        solved_send(0, j)
    wide_local(1).wait()
    core_wait(late[0], 0)
    part = mm(fac[1, i, SLOT[0]], first[...])

    @pl.when(k >= 1)
    def _():
        up_copy().wait_recv()

    part = part + mm(fac[1, i, SLOT[4]], below[...])
    shifted[...] = (wide[1].astype(F32) - part).astype(BF16)
    deal_start(1)
    forward(1)
    begin(3)
    finish_diag(0)
    finish_diag(1)
    forward(2)
    for l in range(1, top):
        deal_wait(l)
        for p in (2 * l - 2, 2 * l - 1):
            for source in range(GROUP):
                core_wait(p, source)
        solved_recv(l - 1)
        solve_level(l)
        if l == 1:
            for j in range(GROUP):
                solved_t[0, j] = win[0, REACH + j].astype(F32).T.astype(BF16)
        forward(2 * l + 1)
        if l + 1 < top:
            for p in (2 * l, 2 * l + 1):
                finish_diag(p)
            forward(2 * l + 2)

    deal_wait(top)
    solved_recv(top - 1)
    for source in range(GROUP):
        if source == 3:
            for p in (2 * top - 2, 2 * top - 1):
                finish_diag(p)
            for p in late:
                start(p)
        for p in (2 * top - 2, 2 * top - 1):
            core_wait(p, source)
        j = sources[source]
        adjusted = solve(top, j).T.astype(BF16)
        samp_t[top, j] = mm(adjusted, fac[top, j, DIAG]).astype(BF16)

    def term_copy(l, n):
        dst = far.at[l] if n == 0 else near.at[l, n - 1]
        return remote(stage.at[l, n], dst, s_b.at[l, n], r_b.at[l, n], at(me - GROUP, c))

    def out_copy(l, n, q):
        return remote(
            ostage.at[l, q], out.at[l, 0, :, columns(i)], s_o.at[l, n], r_o.at[l, n], at(base + q, c)
        )

    def out_local(l):
        return pltpu.make_async_copy(ostage.at[l, i], out.at[l, 0, :, columns(i)], s_o.at[l, 3])

    def emit(l, j):
        ostage[l, j] = samp_t[l, j].astype(F32).T.astype(BF16)
        jx, jy = j % 2, j // 2
        ix, iy = i % 2, i // 2
        n = 2 * (iy + jy - 2 * iy * jy) + (ix + jx - 2 * ix * jx) - 1

        @pl.when(i == j)
        def _():
            out_local(l).start()

        @pl.when(i != j)
        def _():
            out_copy(l, n, j).start()

    def terms(l, w):
        total = None
        for j in range(max(0, w - REACH), min(GROUP - 1, w) + 1):
            term = mm(samp_t[l + 1, j], fac[l + 1, j, SLOT[REACH + j - w]])
            total = term if total is None else total + term
        return total

    def ship(l, w):
        total = terms(l, w)
        if w == REACH - 1:
            @pl.when((k + 1 < planes) & (k >= 1))
            def _():
                term_copy(l, 0).wait_recv()

            total = total + far[l].astype(F32)
        stage[l, w] = total.astype(BF16)

        @pl.when(k >= (2 if w == 0 else 1))
        def _():
            term_copy(l, w).start()

    for w in range(REACH):
        ship(top - 1, w)
    for l in range(top - 1, -1, -1):
        for j in range(GROUP):
            emit(l + 1, j)
        back = [terms(l, REACH + j) for j in range(GROUP)]
        for j in range(GROUP):
            @pl.when(k + 1 < planes)
            def _():
                term_copy(l, j + 1).wait_recv()

            total = back[j] + near[l, j].astype(F32)
            adjusted = (solved_t[l, j].astype(F32) - total).astype(BF16)
            samp_t[l, j] = mm(adjusted, fac[l, j, DIAG]).astype(BF16)
            if l > 0:
                for w in range(REACH):
                    if min(GROUP - 1, w) == j:
                        ship(l - 1, w)
            else:
                emit(l, j)
            if l == top - 1 and j == 1:
                for p in late:
                    forward(p)
        if l == top - 1:
            for p in late:
                finish_diag(p)
            for p in late:
                for source in range(1, GROUP):
                    core_wait(p, source)

    for p in range(len(parts)):
        for n in range(2):
            own_copy(p, n).wait_send()
            diag_copy(p, n).wait_send()
        for source in range(GROUP):
            for r in cores:
                core_copy(p, source, r).wait_send()
    for t in range(levels):
        for n in range(3):
            deal_copy(t, n).wait_send()

    @pl.when(k + 1 < planes)
    def _():
        up_copy().wait_send()

    for l in range(levels - 1):
        @pl.when(k + 1 < planes)
        def _():
            for n in range(GROUP):
                solved_copy(l, n).wait_send()

        @pl.when(k + 2 < planes)
        def _():
            solved_copy(l, GROUP).wait_send()

        @pl.when(k >= 1)
        def _():
            for n in range(1, REACH):
                term_copy(l, n).wait_send()

        @pl.when(k >= 2)
        def _():
            term_copy(l, 0).wait_send()

    for l in range(levels):
        for n in range(3):
            out_copy(l, n, peers[n]).wait()
        out_local(l).wait()


def on_device(rhs, blocks, diag_inv, neighbours):
    owners = lax.axis_size("sweep")
    ncores = lax.axis_size("cols")
    levels, _, bs, cols = rhs.shape
    width = cols // GROUP
    parts = len(parts_of(levels)[0])
    dma = pltpu.SemaphoreType.DMA
    hbm = pl.BlockSpec(memory_space=pltpu.HBM)
    return pl.pallas_call(
        functools.partial(kernel, owners, ncores),
        out_shape=jax.ShapeDtypeStruct(rhs.shape, rhs.dtype),
        in_specs=[pl.BlockSpec(memory_space=pltpu.SMEM), hbm, hbm, hbm],
        out_specs=hbm,
        scratch_shapes=[
            pltpu.VMEM((levels, GROUP, REACH + 2, bs, bs), BF16),
            pltpu.VMEM(blocks.shape[:1] + blocks.shape[2:], BF16),
            pltpu.VMEM((2, bs, cols), BF16),
            pltpu.VMEM((bs, cols), BF16),
            pltpu.VMEM((bs, cols), BF16),
            pltpu.VMEM((bs, cols), BF16),
            pltpu.VMEM((levels - 1, REACH + GROUP, bs, width), BF16),
            pltpu.VMEM((levels, GROUP, bs, width), BF16),
            pltpu.VMEM((levels, GROUP, width, bs), BF16),
            pltpu.VMEM((levels, GROUP, width, bs), BF16),
            pltpu.VMEM((levels - 1, GROUP, width, bs), BF16),
            pltpu.VMEM((levels - 1, width, bs), BF16),
            pltpu.VMEM((levels - 1, REACH, width, bs), BF16),
            pltpu.VMEM((levels, GROUP, bs, width), BF16),
            dma((parts, 2)), dma((parts, 2)),
            dma((parts, 2)), dma((parts, 2)),
            dma((parts, 4, ncores - 1)), dma((parts, 4, ncores - 1)),
            dma((levels, 3)), dma((levels, 3)), dma((levels,)),
            dma, dma,
            dma((levels - 1, REACH)), dma((levels - 1, REACH)),
            dma((levels - 1, REACH)), dma((levels - 1, REACH)),
            dma((levels, 4)), dma((levels, 3)), dma, dma((levels,)), dma((2,)),
        ],
        compiler_params=pltpu.CompilerParams(
            collective_id=0, has_side_effects=True, vmem_limit_bytes=62 << 20
        ),
    )(neighbours, rhs, blocks, diag_inv)


def solution(mesh):
    placed = (
        P(None, "sweep", None, "cols"),
        P(None, "sweep", None, "cols", None),
        P(None, "sweep", "cols", None),
        P(None, "sweep", None),
    )
    return jax.shard_map(
        on_device,
        mesh=mesh,
        in_specs=placed,
        out_specs=P(None, "sweep", None, "cols"),
        check_vma=False,
    )
```

```python
import functools

import jax
import jax.numpy as jnp
from jax import lax
from jax.experimental import pallas as pl
from jax.experimental.pallas import tpu as pltpu
from jax.sharding import PartitionSpec as P

REACH = 5
GROUP = 4
F32 = jnp.float32
BF16 = jnp.bfloat16

SLOT = {0: 0, 4: 1, 1: 2, 2: 3, 3: 4, 5: 5}
DIAG = REACH + 1


def parts_of(levels):
    early = [(1, 2, 2), (1, 4, 3)]
    for t in range(2, levels):
        early += [(t, 0, 4), (t, 4, 3)]
    return early + [(1, 0, 2), (0, DIAG, 1)], len(early)


def mm(a, b):
    return jnp.dot(a, b, preferred_element_type=F32)


def kernel(
    owners, ncores, nbr, rhs, blocks, diag, out,
    fac, raw, wide, first, below, shifted, win, rloc, solved_t, samp_t, near, far, stage, ostage,
    s_own, r_own, s_dg, r_dg, s_core, r_core, s_rhs, r_rhs, s_loc,
    s_up, r_up, s_x, r_x, s_b, r_b, s_o, r_o, s_raw, s_diag, s_wide,
):
    levels = rhs.shape[0]
    rows = diag.shape[2]
    slots = blocks.shape[2]
    width = rhs.shape[3] // GROUP
    planes = owners // GROUP
    top = levels - 1
    parts, n_early = parts_of(levels)
    me = lax.axis_index("sweep")
    c = lax.axis_index("cols")
    k = me // GROUP
    i = me % GROUP
    px = i + 1 - 2 * (i % 2)
    py = (i + 2) % GROUP
    dg = GROUP - 1 - i
    base = k * GROUP
    peers = (px, py, dg)
    sources = (i,) + peers
    cores = range(1, ncores)

    def at(owner, core):
        return (owner, core)

    def remote(src, dst, ssem, rsem, dev):
        return pltpu.make_async_remote_copy(
            src_ref=src, dst_ref=dst, send_sem=ssem, recv_sem=rsem,
            device_id=dev, device_id_type=pl.DeviceIdType.MESH,
        )

    barrier = pltpu.get_barrier_semaphore()

    def greet(owner, core):
        pl.semaphore_signal(
            barrier, inc=1, device_id=at(owner, core), device_id_type=pl.DeviceIdType.MESH
        )

    for q in peers:
        greet(base + q, c)
    for r in range(1, ncores):
        greet(me, (c + r) % ncores)
    count = 3 + ncores - 1
    for d in (1, 2):
        @pl.when(k >= d)
        def _():
            greet(me - d * GROUP, c)

        @pl.when(k + d < planes)
        def _():
            greet(me + d * GROUP, c)

        count = count + jnp.where(k >= d, 1, 0) + jnp.where(k + d < planes, 1, 0)

    mine = pl.ds(pl.multiple_of(c * rows, rows), rows)

    def diag_local(t):
        return pltpu.make_async_copy(diag.at[t, 0], fac.at[t, i, DIAG, mine, :], s_diag.at[t])

    def wide_local(t):
        return pltpu.make_async_copy(rhs.at[t, 0], wide.at[t], s_wide.at[t])

    raw_local = pltpu.make_async_copy(blocks.at[:, 0], raw, s_raw)
    diag_local(0).start()
    raw_local.start()
    for t in range(2):
        wide_local(t).start()
    for t in range(1, levels):
        diag_local(t).start()

    def clear(ref):
        ref[...] = jnp.zeros_like(ref)

    @pl.when(k == 0)
    def _():
        clear(below)
        for l in range(levels - 1):
            clear(win.at[l, 0:REACH])

    @pl.when(k == 1)
    def _():
        for l in range(levels - 1):
            clear(win.at[l, 0])

    @pl.when(k + 1 >= planes)
    def _():
        clear(near)

    @pl.when((k + 1 >= planes) | (k < 1))
    def _():
        clear(far)

    def stage_level(t):
        for o in range(REACH + 1):
            slot, hit = jnp.int32(0), jnp.int32(0)
            for s in range(slots):
                got = nbr[t - 1, 0, s]
                same = (got == (t - 1) * owners + me - o) & (got >= 0)
                slot = jnp.where(same, s, slot)
                hit = jnp.where(same, 1, hit)
            block = raw[t - 1, slot].astype(F32) * hit.astype(F32)
            fac[t, i, SLOT[o], mine, :] = block.astype(BF16)
        diag_local(t).wait()

    half = rows // 2

    def shard(p, owner):
        t, lo, n = parts[p]
        return fac.at[t, owner, pl.ds(lo, n), mine, :]

    def shard_half(p, owner, h):
        t, lo, n = parts[p]
        part = pl.ds(pl.multiple_of(c * rows + h * half, half), half)
        return fac.at[t, owner, pl.ds(lo, n), part, :]

    def own_copy(p, n):
        ref = shard(p, i)
        return remote(ref, ref, s_own.at[p, n], r_own.at[p, n], at(base + peers[n], c))

    def diag_copy(p, n):
        ref = shard_half(p, peers[n], n)
        return remote(ref, ref, s_dg.at[p, n], r_dg.at[p, n], at(base + peers[1 - n], c))

    def core_copy(p, source, r):
        ref = shard(p, sources[source])
        return remote(
            ref, ref, s_core.at[p, source, r - 1], r_core.at[p, source, r - 1],
            at(me, (c + r) % ncores),
        )

    def columns(q):
        return pl.ds(pl.multiple_of(q * width, width), width)

    def deal(t, q):
        if t == 0:
            return first.at[:, columns(q)], win.at[0, REACH + i]
        if t == 1:
            return shifted.at[:, columns(q)], rloc.at[1, i]
        return rhs.at[t, 0, :, columns(q)], rloc.at[t, i]

    def deal_copy(t, n):
        src, dst = deal(t, peers[n])
        return remote(src, dst, s_rhs.at[t, n], r_rhs.at[t, n], at(base + peers[n], c))

    def deal_local(t):
        src, dst = deal(t, i)
        return pltpu.make_async_copy(src, dst, s_loc.at[t])

    def deal_start(t):
        for n in range(3):
            deal_copy(t, n).start()
        deal_local(t).start()

    def deal_wait(t):
        for n in range(3):
            deal_copy(t, n).wait_recv()
        deal_local(t).wait()

    def core_start(p, source):
        for r in cores:
            core_copy(p, source, r).start()

    def core_wait(p, source):
        for r in cores:
            core_copy(p, source, r).wait_recv()

    def start(p):
        for n in range(2):
            own_copy(p, n).start()

    def forward(p):
        for n in range(2):
            own_copy(p, n).wait_recv()
            diag_copy(p, n).start()
            core_start(p, 1 + n)

    def finish_diag(p):
        for n in range(2):
            diag_copy(p, n).wait_recv()
        core_start(p, 3)

    def up_copy():
        return remote(first, below, s_up, r_up, at(me + GROUP, c))

    def solved_copy(l, n):
        j = GROUP - 1 if n == GROUP else n
        step, spot = (2, 0) if n == GROUP else (1, 1 + n)
        return remote(
            win.at[l, REACH + j], win.at[l, spot], s_x.at[l, n], r_x.at[l, n],
            at(me + step * GROUP, c),
        )

    def solved_send(l, j):
        @pl.when(k + 1 < planes)
        def _():
            solved_copy(l, j).start()

        if j == GROUP - 1:
            @pl.when(k + 2 < planes)
            def _():
                solved_copy(l, GROUP).start()

    def solved_recv(l):
        @pl.when(k >= 1)
        def _():
            for n in range(GROUP):
                solved_copy(l, n).wait_recv()

        @pl.when(k >= 2)
        def _():
            solved_copy(l, GROUP).wait_recv()

    def solve(l, j):
        acc = None
        for o in range(REACH + 1):
            if l == 1 and SLOT[o] < 2:
                continue
            term = mm(fac[l, j, SLOT[o]], win[l - 1, REACH + j - o])
            acc = term if acc is None else acc + term
        res = (rloc[l, j].astype(F32) - acc).astype(BF16)
        return mm(fac[l, j, DIAG], res)

    def solve_level(l):
        for j in reversed(range(GROUP)):
            y = solve(l, j)
            win[l, REACH + j] = y.astype(BF16)
            solved_send(l, j)
            solved_t[l, j] = y.T.astype(BF16)

    late = (n_early, n_early + 1)
    raw_local.wait()
    stage_level(1)
    diag_local(0).wait()
    pl.semaphore_wait(barrier, count)

    core_start(late[1], 0)
    core_start(late[0], 0)
    start(0)
    core_start(0, 0)
    core_start(1, 0)
    wide_local(0).wait()
    core_wait(late[1], 0)
    first[...] = mm(fac[0, i, DIAG], wide[0]).astype(BF16)
    deal_start(0)

    @pl.when(k + 1 < planes)
    def _():
        up_copy().start()

    start(1)
    wide_local(1).wait()
    core_wait(late[0], 0)
    for t in range(2, levels):
        stage_level(t)
        for p in (2 * t - 2, 2 * t - 1):
            core_start(p, 0)
    forward(0)
    deal_wait(0)
    for j in reversed(range(GROUP)):
        solved_send(0, j)

    @pl.when(k >= 1)
    def _():
        up_copy().wait_recv()

    part = mm(fac[1, i, SLOT[0]], first[...]) + mm(fac[1, i, SLOT[4]], below[...])
    shifted[...] = (wide[1].astype(F32) - part).astype(BF16)
    deal_start(1)
    for j in range(GROUP):
        solved_t[0, j] = win[0, REACH + j].astype(F32).T.astype(BF16)
    forward(1)
    for l in range(1, top):
        deal_start(l + 1)
        start(2 * l)
        start(2 * l + 1)
        finish_diag(2 * l - 2)
        finish_diag(2 * l - 1)
        deal_wait(l)
        for p in (2 * l - 2, 2 * l - 1):
            for source in range(GROUP):
                core_wait(p, source)
        solved_recv(l - 1)
        solve_level(l)
        forward(2 * l)
        forward(2 * l + 1)

    for p in late:
        start(p)
    deal_wait(top)
    solved_recv(top - 1)
    for source in range(GROUP):
        if source == 3:
            for p in (2 * top - 2, 2 * top - 1):
                finish_diag(p)
        for p in (2 * top - 2, 2 * top - 1):
            core_wait(p, source)
        j = sources[source]
        adjusted = solve(top, j).T.astype(BF16)
        samp_t[top, j] = mm(adjusted, fac[top, j, DIAG]).astype(BF16)

    def term_copy(l, n):
        dst = far.at[l] if n == 0 else near.at[l, n - 1]
        return remote(stage.at[l, n], dst, s_b.at[l, n], r_b.at[l, n], at(me - GROUP, c))

    def out_copy(l, n, q):
        return remote(
            ostage.at[l, q], out.at[l, 0, :, columns(i)], s_o.at[l, n], r_o.at[l, n], at(base + q, c)
        )

    def out_local(l):
        return pltpu.make_async_copy(ostage.at[l, i], out.at[l, 0, :, columns(i)], s_o.at[l, 3])

    def emit(l, j):
        ostage[l, j] = samp_t[l, j].astype(F32).T.astype(BF16)
        jx, jy = j % 2, j // 2
        ix, iy = i % 2, i // 2
        n = 2 * (iy + jy - 2 * iy * jy) + (ix + jx - 2 * ix * jx) - 1

        @pl.when(i == j)
        def _():
            out_local(l).start()

        @pl.when(i != j)
        def _():
            out_copy(l, n, j).start()

    def terms(l, w):
        total = None
        for j in range(max(0, w - REACH), min(GROUP - 1, w) + 1):
            term = mm(samp_t[l + 1, j], fac[l + 1, j, SLOT[REACH + j - w]])
            total = term if total is None else total + term
        return total

    def ship(l, w):
        total = terms(l, w)
        if w == REACH - 1:
            @pl.when((k + 1 < planes) & (k >= 1))
            def _():
                term_copy(l, 0).wait_recv()

            total = total + far[l].astype(F32)
        stage[l, w] = total.astype(BF16)

        @pl.when(k >= (2 if w == 0 else 1))
        def _():
            term_copy(l, w).start()

    for w in range(REACH):
        ship(top - 1, w)
    for l in range(top - 1, -1, -1):
        for j in range(GROUP):
            emit(l + 1, j)
        back = [terms(l, REACH + j) for j in range(GROUP)]
        for j in range(GROUP):
            @pl.when(k + 1 < planes)
            def _():
                term_copy(l, j + 1).wait_recv()

            total = back[j] + near[l, j].astype(F32)
            adjusted = (solved_t[l, j].astype(F32) - total).astype(BF16)
            samp_t[l, j] = mm(adjusted, fac[l, j, DIAG]).astype(BF16)
            if l > 0:
                for w in range(REACH):
                    if min(GROUP - 1, w) == j:
                        ship(l - 1, w)
            else:
                emit(l, j)
            if l == top - 1 and j == 1:
                for p in late:
                    forward(p)
        if l == top - 1:
            for p in late:
                finish_diag(p)
            for p in late:
                for source in range(1, GROUP):
                    core_wait(p, source)

    for p in range(len(parts)):
        for n in range(2):
            own_copy(p, n).wait_send()
            diag_copy(p, n).wait_send()
        for source in range(GROUP):
            for r in cores:
                core_copy(p, source, r).wait_send()
    for t in range(levels):
        for n in range(3):
            deal_copy(t, n).wait_send()

    @pl.when(k + 1 < planes)
    def _():
        up_copy().wait_send()

    for l in range(levels - 1):
        @pl.when(k + 1 < planes)
        def _():
            for n in range(GROUP):
                solved_copy(l, n).wait_send()

        @pl.when(k + 2 < planes)
        def _():
            solved_copy(l, GROUP).wait_send()

        @pl.when(k >= 1)
        def _():
            for n in range(1, REACH):
                term_copy(l, n).wait_send()

        @pl.when(k >= 2)
        def _():
            term_copy(l, 0).wait_send()

    for l in range(levels):
        for n in range(3):
            out_copy(l, n, peers[n]).wait()
        out_local(l).wait()


def on_device(rhs, blocks, diag_inv, neighbours):
    owners = lax.axis_size("sweep")
    ncores = lax.axis_size("cols")
    levels, _, bs, cols = rhs.shape
    width = cols // GROUP
    parts = len(parts_of(levels)[0])
    dma = pltpu.SemaphoreType.DMA
    hbm = pl.BlockSpec(memory_space=pltpu.HBM)
    return pl.pallas_call(
        functools.partial(kernel, owners, ncores),
        out_shape=jax.ShapeDtypeStruct(rhs.shape, rhs.dtype),
        in_specs=[pl.BlockSpec(memory_space=pltpu.SMEM), hbm, hbm, hbm],
        out_specs=hbm,
        scratch_shapes=[
            pltpu.VMEM((levels, GROUP, REACH + 2, bs, bs), BF16),
            pltpu.VMEM(blocks.shape[:1] + blocks.shape[2:], BF16),
            pltpu.VMEM((2, bs, cols), BF16),
            pltpu.VMEM((bs, cols), BF16),
            pltpu.VMEM((bs, cols), BF16),
            pltpu.VMEM((bs, cols), BF16),
            pltpu.VMEM((levels - 1, REACH + GROUP, bs, width), BF16),
            pltpu.VMEM((levels, GROUP, bs, width), BF16),
            pltpu.VMEM((levels, GROUP, width, bs), BF16),
            pltpu.VMEM((levels, GROUP, width, bs), BF16),
            pltpu.VMEM((levels - 1, GROUP, width, bs), BF16),
            pltpu.VMEM((levels - 1, width, bs), BF16),
            pltpu.VMEM((levels - 1, REACH, width, bs), BF16),
            pltpu.VMEM((levels, GROUP, bs, width), BF16),
            dma((parts, 2)), dma((parts, 2)),
            dma((parts, 2)), dma((parts, 2)),
            dma((parts, 4, ncores - 1)), dma((parts, 4, ncores - 1)),
            dma((levels, 3)), dma((levels, 3)), dma((levels,)),
            dma, dma,
            dma((levels - 1, REACH)), dma((levels - 1, REACH)),
            dma((levels - 1, REACH)), dma((levels - 1, REACH)),
            dma((levels, 4)), dma((levels, 3)), dma, dma((levels,)), dma((2,)),
        ],
        compiler_params=pltpu.CompilerParams(
            collective_id=0, has_side_effects=True, vmem_limit_bytes=62 << 20
        ),
    )(neighbours, rhs, blocks, diag_inv)


def solution(mesh):
    placed = (
        P(None, "sweep", None, "cols"),
        P(None, "sweep", None, "cols", None),
        P(None, "sweep", "cols", None),
        P(None, "sweep", None),
    )
    return jax.shard_map(
        on_device,
        mesh=mesh,
        in_specs=placed,
        out_specs=P(None, "sweep", None, "cols"),
        check_vma=False,
    )
```

```python
import functools

import jax
import jax.numpy as jnp
from jax import lax
from jax.experimental import pallas as pl
from jax.experimental.pallas import tpu as pltpu
from jax.sharding import PartitionSpec as P

REACH = 5
GROUP = 4
F32 = jnp.float32
BF16 = jnp.bfloat16

SLOT = {0: 0, 4: 1, 1: 2, 2: 3, 3: 4, 5: 5}
DIAG = REACH + 1


def parts_of(levels):
    early = [(1, 2, 2), (1, 4, 3)]
    for t in range(2, levels):
        early += [(t, 0, 4), (t, 4, 3)]
    return early + [(1, 0, 2), (0, DIAG, 1)], len(early)


def mm(a, b):
    return jnp.dot(a, b, preferred_element_type=F32)


def kernel(
    owners, ncores, neighbours, rhs, blocks, diag, out,
    nbr, fac, raw, wide, first, below, shifted, win, rloc, solved_t, samp_t, near, far, stage, ostage,
    s_own, r_own, s_dg, r_dg, s_core, r_core, s_rhs, r_rhs,
    s_up, r_up, s_x, r_x, s_b, r_b, s_o, r_o, s_raw, s_diag, s_wide, s_nbr,
):
    levels = rhs.shape[0]
    rows = diag.shape[2]
    slots = blocks.shape[2]
    width = rhs.shape[3] // GROUP
    planes = owners // GROUP
    top = levels - 1
    parts, n_early = parts_of(levels)
    me = lax.axis_index("sweep")
    c = lax.axis_index("cols")
    k = me // GROUP
    i = me % GROUP
    px = i + 1 - 2 * (i % 2)
    py = (i + 2) % GROUP
    dg = GROUP - 1 - i
    base = k * GROUP
    peers = (px, py, dg)
    sources = (i,) + peers
    cores = range(1, ncores)

    def at(owner, core):
        return (owner, core)

    def remote(src, dst, ssem, rsem, dev):
        return pltpu.make_async_remote_copy(
            src_ref=src, dst_ref=dst, send_sem=ssem, recv_sem=rsem,
            device_id=dev, device_id_type=pl.DeviceIdType.MESH,
        )

    barrier = pltpu.get_barrier_semaphore()

    def greet(owner, core):
        pl.semaphore_signal(
            barrier, inc=1, device_id=at(owner, core), device_id_type=pl.DeviceIdType.MESH
        )

    for q in peers:
        greet(base + q, c)
    for r in range(1, ncores):
        greet(me, (c + r) % ncores)
    count = 3 + ncores - 1
    for d in (1, 2):
        @pl.when(k >= d)
        def _():
            greet(me - d * GROUP, c)

        @pl.when(k + d < planes)
        def _():
            greet(me + d * GROUP, c)

        count = count + jnp.where(k >= d, 1, 0) + jnp.where(k + d < planes, 1, 0)

    mine = pl.ds(pl.multiple_of(c * rows, rows), rows)

    nbr_local = pltpu.make_async_copy(neighbours, nbr, s_nbr)
    raw_local = pltpu.make_async_copy(blocks.at[:, 0], raw, s_raw)
    diag_first = pltpu.make_async_copy(diag.at[0, 0], fac.at[0, i, DIAG, mine, :], s_diag.at[0])
    diag_rest = pltpu.make_async_copy(
        diag.at[1:, 0], fac.at[pl.ds(1, top), i, DIAG, mine, :], s_diag.at[1]
    )
    wide_local = pltpu.make_async_copy(rhs.at[0:2, 0], wide, s_wide)
    for local in (nbr_local, diag_first, raw_local, wide_local, diag_rest):
        local.start()

    def clear(ref):
        ref[...] = jnp.zeros_like(ref)

    @pl.when(k == 0)
    def _():
        clear(below)
        for l in range(levels - 1):
            clear(win.at[l, 0:REACH])

    @pl.when(k == 1)
    def _():
        for l in range(levels - 1):
            clear(win.at[l, 0])

    @pl.when(k + 1 >= planes)
    def _():
        clear(near)

    @pl.when((k + 1 >= planes) | (k < 1))
    def _():
        clear(far)

    def stage_level(t):
        for o in range(REACH + 1):
            slot, hit = jnp.int32(0), jnp.int32(0)
            for s in range(slots):
                got = nbr[t - 1, 0, s]
                same = (got == (t - 1) * owners + me - o) & (got >= 0)
                slot = jnp.where(same, s, slot)
                hit = jnp.where(same, 1, hit)
            block = raw[t - 1, slot].astype(F32) * hit.astype(F32)
            fac[t, i, SLOT[o], mine, :] = block.astype(BF16)

    half = rows // 2

    def shard(p, owner):
        t, lo, n = parts[p]
        return fac.at[t, owner, pl.ds(lo, n), mine, :]

    def shard_half(p, owner, h):
        t, lo, n = parts[p]
        part = pl.ds(pl.multiple_of(c * rows + h * half, half), half)
        return fac.at[t, owner, pl.ds(lo, n), part, :]

    def settle(ref, sem):
        pltpu.make_async_copy(ref, ref, sem).wait()

    def spot_of(p):
        return parts[p][0] - 1 if p < n_early else top + p - n_early

    def core_spot(p, source):
        if p >= n_early:
            return top + GROUP - 1 + 2 * (p - n_early) + (1 if source else 0)
        t = parts[p][0]
        return t - 1 if t < top else top - 1 + source

    def own_copy(p, n):
        ref = shard(p, i)
        return remote(ref, ref, s_own.at[spot_of(p)], r_own.at[p, n], at(base + peers[n], c))

    def diag_copy(p, n):
        ref = shard_half(p, peers[n], n)
        return remote(ref, ref, s_dg.at[spot_of(p)], r_dg.at[p], at(base + peers[1 - n], c))

    def core_copy(p, source, r):
        ref = shard(p, sources[source])
        return remote(
            ref, ref, s_core.at[spot_of(p), r - 1], r_core.at[core_spot(p, source), r - 1],
            at(me, (c + r) % ncores),
        )

    def span(t, first_slot, n, count):
        return fac.at[t, pl.ds(0, count), pl.ds(first_slot, n), mine, :]

    def columns(q):
        return pl.ds(pl.multiple_of(q * width, width), width)

    def deal(t, q):
        if t == 0:
            return first.at[:, columns(q)], win.at[0, REACH + i]
        if t == 1:
            return shifted.at[:, columns(q)], rloc.at[1, i]
        return rhs.at[t, 0, :, columns(q)], rloc.at[t, i]

    def deal_copy(t, n):
        src, dst = deal(t, peers[n])
        return remote(src, dst, s_rhs, r_rhs.at[t], at(base + peers[n], c))

    def deal_local(t):
        src, dst = deal(t, i)
        return pltpu.make_async_copy(src, dst, r_rhs.at[t])

    def deal_start(t):
        for n in range(3):
            deal_copy(t, n).start()
        deal_local(t).start()

    def deal_wait(t):
        settle(win.at[0, pl.ds(REACH, GROUP)] if t == 0 else rloc.at[t], r_rhs.at[t])

    def core_start(p, source):
        for r in cores:
            core_copy(p, source, r).start()

    def core_wait(p, source, ref):
        for r in cores:
            settle(ref, r_core.at[core_spot(p, source), r - 1])

    def start(p):
        for n in range(2):
            own_copy(p, n).start()

    def forward(p):
        for n in range(2):
            own_copy(p, n).wait_recv()
            diag_copy(p, n).start()
            core_start(p, 1 + n)

    def finish_diag(p):
        settle(shard(p, i), r_dg.at[p])
        core_start(p, 3)

    def up_copy():
        return remote(first, below, s_up, r_up, at(me + GROUP, c))

    def solved_copy(l, n):
        j = GROUP - 1 if n == GROUP else n
        step, spot = (2, 0) if n == GROUP else (1, 1 + n)
        return remote(
            win.at[l, REACH + j], win.at[l, spot], s_x.at[step - 1], r_x.at[l, step - 1],
            at(me + step * GROUP, c),
        )

    def solved_send(l, j):
        @pl.when(k + 1 < planes)
        def _():
            solved_copy(l, j).start()

        if j == GROUP - 1:
            @pl.when(k + 2 < planes)
            def _():
                solved_copy(l, GROUP).start()

    def solved_recv(l):
        @pl.when(k >= 1)
        def _():
            settle(win.at[l, pl.ds(1, GROUP)], r_x.at[l, 0])

        @pl.when(k >= 2)
        def _():
            settle(win.at[l, 0], r_x.at[l, 1])

    def solve(l, j):
        acc = None
        for o in range(REACH + 1):
            if l == 1 and SLOT[o] < 2:
                continue
            term = mm(fac[l, j, SLOT[o]], win[l - 1, REACH + j - o])
            acc = term if acc is None else acc + term
        res = (rloc[l, j].astype(F32) - acc).astype(BF16)
        return mm(fac[l, j, DIAG], res)

    def solve_level(l):
        for j in reversed(range(GROUP)):
            y = solve(l, j)
            win[l, REACH + j] = y.astype(BF16)
            solved_send(l, j)
            solved_t[l, j] = y.T.astype(BF16)

    late = (n_early, n_early + 1)
    nbr_local.wait()
    raw_local.wait()
    stage_level(1)
    diag_first.wait()
    diag_rest.wait()
    pl.semaphore_wait(barrier, count)

    core_start(late[1], 0)
    core_start(late[0], 0)
    start(0)
    core_start(0, 0)
    core_start(1, 0)
    wide_local.wait()
    core_wait(late[1], 0, shard(late[1], i))
    first[...] = mm(fac[0, i, DIAG], wide[0]).astype(BF16)
    deal_start(0)

    @pl.when(k + 1 < planes)
    def _():
        up_copy().start()

    start(1)
    core_wait(late[0], 0, shard(late[0], i))
    for t in range(2, levels):
        stage_level(t)
        for p in (2 * t - 2, 2 * t - 1):
            core_start(p, 0)
    forward(0)
    deal_wait(0)
    for j in reversed(range(GROUP)):
        solved_send(0, j)

    @pl.when(k >= 1)
    def _():
        up_copy().wait_recv()

    part = mm(fac[1, i, SLOT[0]], first[...]) + mm(fac[1, i, SLOT[4]], below[...])
    shifted[...] = (wide[1].astype(F32) - part).astype(BF16)
    deal_start(1)
    for j in range(GROUP):
        solved_t[0, j] = win[0, REACH + j].astype(F32).T.astype(BF16)
    forward(1)
    for l in range(1, top):
        deal_start(l + 1)
        start(2 * l)
        start(2 * l + 1)
        finish_diag(2 * l - 2)
        finish_diag(2 * l - 1)
        deal_wait(l)
        lo = 2 if l == 1 else 0
        core_wait(2 * l - 2, 0, span(l, lo, DIAG + 1 - lo, GROUP))
        solved_recv(l - 1)
        solve_level(l)
        forward(2 * l)
        forward(2 * l + 1)

    for p in late:
        start(p)
    deal_wait(top)
    solved_recv(top - 1)
    for source in range(GROUP):
        if source == 3:
            for p in (2 * top - 2, 2 * top - 1):
                finish_diag(p)
        core_wait(2 * top - 2, source, span(top, 0, DIAG + 1, 1))
        j = sources[source]
        adjusted = solve(top, j).T.astype(BF16)
        samp_t[top, j] = mm(adjusted, fac[top, j, DIAG]).astype(BF16)

    def term_copy(l, n):
        dst = far.at[l] if n == 0 else near.at[l, n - 1]
        return remote(stage.at[l, n], dst, s_b.at[min(n, 1)], r_b.at[l, n], at(me - GROUP, c))

    def out_copy(l, q):
        return remote(
            ostage.at[l, q], out.at[l, 0, :, columns(i)], s_o, r_o, at(base + q, c)
        )

    def out_local(l):
        return pltpu.make_async_copy(ostage.at[l, i], out.at[l, 0, :, columns(i)], s_o)

    def emit(l, j):
        ostage[l, j] = samp_t[l, j].astype(F32).T.astype(BF16)

        @pl.when(i == j)
        def _():
            out_local(l).start()

        @pl.when(i != j)
        def _():
            out_copy(l, j).start()

    def terms(l, w):
        total = None
        for j in range(max(0, w - REACH), min(GROUP - 1, w) + 1):
            term = mm(samp_t[l + 1, j], fac[l + 1, j, SLOT[REACH + j - w]])
            total = term if total is None else total + term
        return total

    def ship(l, w):
        total = terms(l, w)
        if w == REACH - 1:
            @pl.when((k + 1 < planes) & (k >= 1))
            def _():
                term_copy(l, 0).wait_recv()

            total = total + far[l].astype(F32)
        stage[l, w] = total.astype(BF16)

        @pl.when(k >= (2 if w == 0 else 1))
        def _():
            term_copy(l, w).start()

    for w in range(REACH):
        ship(top - 1, w)
    for l in range(top - 1, -1, -1):
        for j in range(GROUP):
            emit(l + 1, j)
        back = [terms(l, REACH + j) for j in range(GROUP)]
        for j in range(GROUP):
            @pl.when(k + 1 < planes)
            def _():
                term_copy(l, j + 1).wait_recv()

            total = back[j] + near[l, j].astype(F32)
            adjusted = (solved_t[l, j].astype(F32) - total).astype(BF16)
            samp_t[l, j] = mm(adjusted, fac[l, j, DIAG]).astype(BF16)
            if l > 0:
                for w in range(REACH):
                    if min(GROUP - 1, w) == j:
                        ship(l - 1, w)
            else:
                emit(l, j)
            if l == top - 1 and j == 1:
                for p in late:
                    forward(p)
        if l == top - 1:
            for p in late:
                finish_diag(p)
            for p in late:
                t, lo, n = parts[p]
                core_wait(p, 1, span(t, lo, n, GROUP - 1))

    sent = [(1, 2, DIAG - 1)] + [(t, 0, DIAG + 1) for t in range(2, levels)]
    sent += [parts[p] for p in late]
    for spot, (t, lo, n) in enumerate(sent):
        settle(span(t, lo, n, 2), s_own.at[spot])
        settle(span(t, lo, n, 1), s_dg.at[spot])
        for r in cores:
            settle(span(t, lo, n, GROUP), s_core.at[spot, r - 1])
    settle(rloc.at[:, pl.ds(0, 3)], s_rhs)

    @pl.when(k + 1 < planes)
    def _():
        settle(first, s_up)
        settle(win.at[:, pl.ds(0, GROUP)], s_x.at[0])

    @pl.when(k + 2 < planes)
    def _():
        settle(win.at[:, 0], s_x.at[1])

    @pl.when(k >= 1)
    def _():
        settle(stage.at[:, pl.ds(1, REACH - 1)], s_b.at[1])

    @pl.when(k >= 2)
    def _():
        settle(stage.at[:, 0], s_b.at[0])

    settle(ostage, s_o)
    settle(ostage.at[:, pl.ds(0, 3)], r_o)


def on_device(rhs, blocks, diag_inv, neighbours):
    owners = lax.axis_size("sweep")
    ncores = lax.axis_size("cols")
    levels, _, bs, cols = rhs.shape
    width = cols // GROUP
    parts = len(parts_of(levels)[0])
    dma = pltpu.SemaphoreType.DMA
    hbm = pl.BlockSpec(memory_space=pltpu.HBM)
    return pl.pallas_call(
        functools.partial(kernel, owners, ncores),
        out_shape=pltpu.VMEM(rhs.shape, rhs.dtype),
        in_specs=[hbm, hbm, hbm, hbm],
        out_specs=pl.BlockSpec(memory_space=pltpu.VMEM),
        scratch_shapes=[
            pltpu.SMEM(neighbours.shape, jnp.int32),
            pltpu.VMEM((levels, GROUP, REACH + 2, bs, bs), BF16),
            pltpu.VMEM(blocks.shape[:1] + blocks.shape[2:], BF16),
            pltpu.VMEM((2, bs, cols), BF16),
            pltpu.VMEM((bs, cols), BF16),
            pltpu.VMEM((bs, cols), BF16),
            pltpu.VMEM((bs, cols), BF16),
            pltpu.VMEM((levels - 1, REACH + GROUP, bs, width), BF16),
            pltpu.VMEM((levels, GROUP, bs, width), BF16),
            pltpu.VMEM((levels, GROUP, width, bs), BF16),
            pltpu.VMEM((levels, GROUP, width, bs), BF16),
            pltpu.VMEM((levels - 1, GROUP, width, bs), BF16),
            pltpu.VMEM((levels - 1, width, bs), BF16),
            pltpu.VMEM((levels - 1, REACH, width, bs), BF16),
            pltpu.VMEM((levels, GROUP, bs, width), BF16),
            dma((levels + 1,)), dma((parts, 2)), dma((levels + 1,)), dma((parts,)),
            dma((levels + 1, ncores - 1)), dma((levels + GROUP + 2, ncores - 1)),
            dma, dma((levels,)), dma, dma,
            dma((2,)), dma((levels - 1, 2)), dma((2,)), dma((levels - 1, REACH)),
            dma, dma, dma, dma((2,)), dma, dma,
        ],
        compiler_params=pltpu.CompilerParams(
            collective_id=0, has_side_effects=True, vmem_limit_bytes=62 << 20
        ),
    )(neighbours, rhs, blocks, diag_inv)


def solution(mesh):
    placed = (
        P(None, "sweep", None, "cols"),
        P(None, "sweep", None, "cols", None),
        P(None, "sweep", "cols", None),
        P(None, "sweep", None),
    )
    return jax.shard_map(
        on_device,
        mesh=mesh,
        in_specs=placed,
        out_specs=P(None, "sweep", None, "cols"),
        check_vma=False,
    )
```

```python
import functools

import jax
import jax.numpy as jnp
from jax import lax
from jax.experimental import pallas as pl
from jax.experimental.pallas import tpu as pltpu
from jax.sharding import PartitionSpec as P

REACH = 5
GROUP = 4
F32 = jnp.float32
BF16 = jnp.bfloat16

SLOT = {0: 0, 4: 1, 1: 2, 2: 3, 3: 4, 5: 5}
DIAG = REACH + 1


def parts_of(levels):
    early = [(1, 2, 2), (1, 4, 2), (1, DIAG, 1)]
    for t in range(2, levels):
        early += [(t, 0, 4), (t, 4, 2), (t, DIAG, 1)]
    return early + [(1, 0, 2), (0, DIAG, 1)], len(early)


def mm(a, b):
    return jnp.dot(a, b, preferred_element_type=F32)


def kernel(
    owners, ncores, neighbours, rhs, blocks, diag, out,
    nbr, fac, raw, wide, first, below, shifted, win, rloc, solved_t, samp_t, near, far, stage, ostage,
    s_own, r_own, s_dg, r_dg, s_core, r_core, s_rhs, r_rhs,
    s_up, r_up, s_x, r_x, s_b, r_b, s_o, r_o, s_raw, s_diag, s_wide, s_nbr,
):
    levels = rhs.shape[0]
    rows = diag.shape[2]
    slots = blocks.shape[2]
    width = rhs.shape[3] // GROUP
    planes = owners // GROUP
    top = levels - 1
    parts, n_early = parts_of(levels)
    me = lax.axis_index("sweep")
    c = lax.axis_index("cols")
    k = me // GROUP
    i = me % GROUP
    px = i + 1 - 2 * (i % 2)
    py = (i + 2) % GROUP
    dg = GROUP - 1 - i
    base = k * GROUP
    peers = (px, py, dg)
    sources = (i,) + peers
    cores = range(1, ncores)

    def at(owner, core):
        return (owner, core)

    def remote(src, dst, ssem, rsem, dev):
        return pltpu.make_async_remote_copy(
            src_ref=src, dst_ref=dst, send_sem=ssem, recv_sem=rsem,
            device_id=dev, device_id_type=pl.DeviceIdType.MESH,
        )

    barrier = pltpu.get_barrier_semaphore()

    def greet(owner, core):
        pl.semaphore_signal(
            barrier, inc=1, device_id=at(owner, core), device_id_type=pl.DeviceIdType.MESH
        )

    for q in peers:
        greet(base + q, c)
    for r in range(1, ncores):
        greet(me, (c + r) % ncores)
    count = 3 + ncores - 1
    for d in (1, 2):
        @pl.when(k >= d)
        def _():
            greet(me - d * GROUP, c)

        @pl.when(k + d < planes)
        def _():
            greet(me + d * GROUP, c)

        count = count + jnp.where(k >= d, 1, 0) + jnp.where(k + d < planes, 1, 0)

    mine = pl.ds(pl.multiple_of(c * rows, rows), rows)

    side = diag.shape[3] // 2
    for t in range(levels):
        for j in range(GROUP):
            fac[t, j, DIAG, 0:side, side:] = jnp.zeros((side, side), BF16)

    nbr_local = pltpu.make_async_copy(neighbours, nbr, s_nbr)
    raw_local = pltpu.make_async_copy(blocks.at[:, 0], raw, s_raw)
    diag_first = pltpu.make_async_copy(diag.at[0, 0], fac.at[0, i, DIAG, mine, :], s_diag.at[0])
    diag_rest = pltpu.make_async_copy(
        diag.at[1:, 0], fac.at[pl.ds(1, top), i, DIAG, mine, :], s_diag.at[1]
    )
    wide_local = pltpu.make_async_copy(rhs.at[0:2, 0], wide, s_wide)
    for local in (nbr_local, diag_first, raw_local, wide_local, diag_rest):
        local.start()

    def clear(ref):
        ref[...] = jnp.zeros_like(ref)

    @pl.when(k == 0)
    def _():
        clear(below)
        for l in range(levels - 1):
            clear(win.at[l, 0:REACH])

    @pl.when(k == 1)
    def _():
        for l in range(levels - 1):
            clear(win.at[l, 0])

    @pl.when(k + 1 >= planes)
    def _():
        clear(near)

    @pl.when((k + 1 >= planes) | (k < 1))
    def _():
        clear(far)

    def stage_level(t):
        for o in range(REACH + 1):
            slot, hit = jnp.int32(0), jnp.int32(0)
            for s in range(slots):
                got = nbr[t - 1, 0, s]
                same = (got == (t - 1) * owners + me - o) & (got >= 0)
                slot = jnp.where(same, s, slot)
                hit = jnp.where(same, 1, hit)
            block = raw[t - 1, slot].astype(F32) * hit.astype(F32)
            fac[t, i, SLOT[o], mine, :] = block.astype(BF16)

    half = rows // 2
    low = 2 * c < ncores

    def is_diag(p):
        return parts[p][1] == DIAG

    def each(p, is_low, act):
        if is_diag(p):
            pl.when(is_low)(lambda: act(side))
            pl.when(jnp.logical_not(is_low))(lambda: act(2 * side))
        else:
            act(2 * side)

    def shard(p, owner, wide_as, count=None):
        t, lo, n = parts[p]
        owner = owner if count is None else pl.ds(owner, count)
        return fac.at[t, owner, pl.ds(lo, n), mine, 0:wide_as]

    def shard_half(p, owner, h, wide_as):
        t, lo, n = parts[p]
        part = pl.ds(pl.multiple_of(c * rows + h * half, half), half)
        return fac.at[t, owner, pl.ds(lo, n), part, 0:wide_as]

    def settle(ref, sem):
        pltpu.make_async_copy(ref, ref, sem).wait()

    def core_spot(p, source):
        d = 1 if is_diag(p) else 0
        if p >= n_early:
            return 2 * (top - 1 + GROUP + d) + (1 if source else 0)
        t = parts[p][0]
        return 2 * (t - 1 if t < top else top - 1 + source) + d

    def own_copy(p, n, w):
        ref = shard(p, i, w)
        return remote(ref, ref, s_own.at[int(is_diag(p))], r_own.at[p, n], at(base + peers[n], c))

    def diag_copy(p, n, w):
        ref = shard_half(p, peers[n], n, w)
        return remote(ref, ref, s_dg.at[int(is_diag(p))], r_dg.at[p], at(base + peers[1 - n], c))

    def core_copy(p, source, r, w):
        ref = shard(p, sources[source], w)
        return remote(
            ref, ref, s_core.at[int(is_diag(p)), r - 1], r_core.at[core_spot(p, source), r - 1],
            at(me, (c + r) % ncores),
        )

    def columns(q):
        return pl.ds(pl.multiple_of(q * width, width), width)

    def deal(t, q):
        if t == 0:
            return first.at[:, columns(q)], win.at[0, REACH + i]
        if t == 1:
            return shifted.at[:, columns(q)], rloc.at[1, i]
        return rhs.at[t, 0, :, columns(q)], rloc.at[t, i]

    def deal_copy(t, n):
        src, dst = deal(t, peers[n])
        return remote(src, dst, s_rhs, r_rhs.at[t], at(base + peers[n], c))

    def deal_local(t):
        src, dst = deal(t, i)
        return pltpu.make_async_copy(src, dst, r_rhs.at[t])

    def deal_start(t):
        for n in range(3):
            deal_copy(t, n).start()
        deal_local(t).start()

    def deal_wait(t):
        settle(win.at[0, pl.ds(REACH, GROUP)] if t == 0 else rloc.at[t], r_rhs.at[t])

    def core_start(p, source):
        for r in cores:
            each(p, low, lambda w: core_copy(p, source, r, w).start())

    def core_wait(p, source, refs):
        for r in cores:
            is_low = 2 * ((c + ncores - r) % ncores) < ncores
            each(p, is_low, lambda w: settle(refs(w), r_core.at[core_spot(p, source), r - 1]))

    def core_wait_level(t, source, first_owner, count):
        p, lo = 3 * t - 3, 2 if t == 1 else 0
        owners_of = pl.ds(first_owner, count)
        core_wait(p, source, lambda w: fac.at[t, owners_of, pl.ds(lo, DIAG - lo), mine, :])

    def start(p):
        for n in range(2):
            each(p, low, lambda w: own_copy(p, n, w).start())

    def forward(p):
        for n in range(2):
            each(p, low, lambda w: own_copy(p, n, w).wait_recv())
            each(p, low, lambda w: diag_copy(p, n, w).start())
            core_start(p, 1 + n)

    def finish_diag(p):
        each(p, low, lambda w: settle(shard(p, i, w), r_dg.at[p]))
        core_start(p, 3)

    def up_copy():
        return remote(first, below, s_up, r_up, at(me + GROUP, c))

    def solved_copy(l, n):
        j = GROUP - 1 if n == GROUP else n
        step, spot = (2, 0) if n == GROUP else (1, 1 + n)
        return remote(
            win.at[l, REACH + j], win.at[l, spot], s_x.at[step - 1], r_x.at[l, step - 1],
            at(me + step * GROUP, c),
        )

    def solved_send(l, j):
        @pl.when(k + 1 < planes)
        def _():
            solved_copy(l, j).start()

        if j == GROUP - 1:
            @pl.when(k + 2 < planes)
            def _():
                solved_copy(l, GROUP).start()

    def solved_recv(l):
        @pl.when(k >= 1)
        def _():
            settle(win.at[l, pl.ds(1, GROUP)], r_x.at[l, 0])

        @pl.when(k >= 2)
        def _():
            settle(win.at[l, 0], r_x.at[l, 1])

    def residue(l, j):
        acc = None
        for o in range(REACH + 1):
            if l == 1 and SLOT[o] < 2:
                continue
            term = mm(fac[l, j, SLOT[o]], win[l - 1, REACH + j - o])
            acc = term if acc is None else acc + term
        return (rloc[l, j].astype(F32) - acc).astype(BF16)

    def solve_level(l):
        for j in reversed(range(GROUP)):
            y = mm(fac[l, j, DIAG], residue(l, j))
            win[l, REACH + j] = y.astype(BF16)
            solved_send(l, j)
            solved_t[l, j] = y.T.astype(BF16)

    late = (n_early, n_early + 1)
    nbr_local.wait()
    raw_local.wait()
    stage_level(1)
    diag_first.wait()
    diag_rest.wait()
    pl.semaphore_wait(barrier, count)

    core_start(late[1], 0)
    core_start(late[0], 0)
    start(0)
    for p in range(3):
        core_start(p, 0)
    wide_local.wait()
    core_wait(late[1], 0, lambda w: shard(late[1], i, w))
    first[...] = mm(fac[0, i, DIAG], wide[0]).astype(BF16)
    deal_start(0)

    @pl.when(k + 1 < planes)
    def _():
        up_copy().start()

    start(1)
    start(2)
    core_wait(late[0], 0, lambda w: shard(late[0], i, w))
    for t in range(2, levels):
        stage_level(t)
        for p in range(3 * t - 3, 3 * t):
            core_start(p, 0)
    forward(0)
    deal_wait(0)
    for j in reversed(range(GROUP)):
        solved_send(0, j)

    @pl.when(k >= 1)
    def _():
        up_copy().wait_recv()

    part = mm(fac[1, i, SLOT[0]], first[...]) + mm(fac[1, i, SLOT[4]], below[...])
    shifted[...] = (wide[1].astype(F32) - part).astype(BF16)
    deal_start(1)
    for j in range(GROUP):
        solved_t[0, j] = win[0, REACH + j].astype(F32).T.astype(BF16)
    forward(1)
    forward(2)
    for l in range(1, top):
        deal_start(l + 1)
        for p in range(3 * l, 3 * l + 3):
            start(p)
        for p in range(3 * l - 3, 3 * l):
            finish_diag(p)
        deal_wait(l)
        core_wait_level(l, 0, 0, GROUP)
        core_wait(3 * l - 1, 0, lambda w: shard(3 * l - 1, 0, w, GROUP))
        solved_recv(l - 1)
        solve_level(l)
        for p in range(3 * l, 3 * l + 3):
            forward(p)

    for p in late:
        start(p)
    deal_wait(top)
    solved_recv(top - 1)
    last = 3 * top - 1
    for source in range(GROUP):
        j = sources[source]
        if source == 3:
            for p in range(last - 2, last + 1):
                finish_diag(p)
        core_wait_level(top, source, 0, 1)
        res = residue(top, j)
        core_wait(last, source, lambda w: shard(last, 0, w))
        adjusted = mm(fac[top, j, DIAG], res).T.astype(BF16)
        samp_t[top, j] = mm(adjusted, fac[top, j, DIAG]).astype(BF16)

    def term_copy(l, n):
        dst = far.at[l] if n == 0 else near.at[l, n - 1]
        return remote(stage.at[l, n], dst, s_b.at[min(n, 1)], r_b.at[l, n], at(me - GROUP, c))

    def out_copy(l, q):
        return remote(
            ostage.at[l, q], out.at[l, 0, :, columns(i)], s_o, r_o, at(base + q, c)
        )

    def out_local(l):
        return pltpu.make_async_copy(ostage.at[l, i], out.at[l, 0, :, columns(i)], s_o)

    def emit(l, j):
        ostage[l, j] = samp_t[l, j].astype(F32).T.astype(BF16)

        @pl.when(i == j)
        def _():
            out_local(l).start()

        @pl.when(i != j)
        def _():
            out_copy(l, j).start()

    def terms(l, w):
        total = None
        for j in range(max(0, w - REACH), min(GROUP - 1, w) + 1):
            term = mm(samp_t[l + 1, j], fac[l + 1, j, SLOT[REACH + j - w]])
            total = term if total is None else total + term
        return total

    def ship(l, w):
        total = terms(l, w)
        if w == REACH - 1:
            @pl.when((k + 1 < planes) & (k >= 1))
            def _():
                term_copy(l, 0).wait_recv()

            total = total + far[l].astype(F32)
        stage[l, w] = total.astype(BF16)

        @pl.when(k >= (2 if w == 0 else 1))
        def _():
            term_copy(l, w).start()

    for w in range(REACH):
        ship(top - 1, w)
    for l in range(top - 1, -1, -1):
        for j in range(GROUP):
            emit(l + 1, j)
        back = [terms(l, REACH + j) for j in range(GROUP)]
        for j in range(GROUP):
            @pl.when(k + 1 < planes)
            def _():
                term_copy(l, j + 1).wait_recv()

            total = back[j] + near[l, j].astype(F32)
            adjusted = (solved_t[l, j].astype(F32) - total).astype(BF16)
            samp_t[l, j] = mm(adjusted, fac[l, j, DIAG]).astype(BF16)
            if l > 0:
                for w in range(REACH):
                    if min(GROUP - 1, w) == j:
                        ship(l - 1, w)
            else:
                emit(l, j)
            if l == top - 1 and j == 1:
                for p in late:
                    forward(p)
        if l == top - 1:
            for p in late:
                finish_diag(p)
            for p in late:
                core_wait(p, 1, lambda w: shard(p, 0, w, GROUP - 1))

    def sent(spot, levels_of, slots_of, w):
        settle(fac.at[levels_of, 0:2, slots_of, mine, 0:w], s_own.at[spot])
        settle(fac.at[levels_of, 0:1, slots_of, mine, 0:w], s_dg.at[spot])
        for r in cores:
            settle(fac.at[levels_of, 0:GROUP, slots_of, mine, 0:w], s_core.at[spot, r - 1])

    sent(0, pl.ds(1, top), pl.ds(0, DIAG), 2 * side)
    each(late[1], low, lambda w: sent(1, pl.ds(0, levels), pl.ds(DIAG, 1), w))
    settle(rloc.at[:, pl.ds(0, 3)], s_rhs)

    @pl.when(k + 1 < planes)
    def _():
        settle(first, s_up)
        settle(win.at[:, pl.ds(0, GROUP)], s_x.at[0])

    @pl.when(k + 2 < planes)
    def _():
        settle(win.at[:, 0], s_x.at[1])

    @pl.when(k >= 1)
    def _():
        settle(stage.at[:, pl.ds(1, REACH - 1)], s_b.at[1])

    @pl.when(k >= 2)
    def _():
        settle(stage.at[:, 0], s_b.at[0])

    settle(ostage, s_o)
    settle(ostage.at[:, pl.ds(0, 3)], r_o)


def on_device(rhs, blocks, diag_inv, neighbours):
    owners = lax.axis_size("sweep")
    ncores = lax.axis_size("cols")
    levels, _, bs, cols = rhs.shape
    width = cols // GROUP
    parts = len(parts_of(levels)[0])
    dma = pltpu.SemaphoreType.DMA
    hbm = pl.BlockSpec(memory_space=pltpu.HBM)
    return pl.pallas_call(
        functools.partial(kernel, owners, ncores),
        out_shape=pltpu.VMEM(rhs.shape, rhs.dtype),
        in_specs=[hbm, hbm, hbm, hbm],
        out_specs=pl.BlockSpec(memory_space=pltpu.VMEM),
        scratch_shapes=[
            pltpu.SMEM(neighbours.shape, jnp.int32),
            pltpu.VMEM((levels, GROUP, REACH + 2, bs, bs), BF16),
            pltpu.VMEM(blocks.shape[:1] + blocks.shape[2:], BF16),
            pltpu.VMEM((2, bs, cols), BF16),
            pltpu.VMEM((bs, cols), BF16),
            pltpu.VMEM((bs, cols), BF16),
            pltpu.VMEM((bs, cols), BF16),
            pltpu.VMEM((levels - 1, REACH + GROUP, bs, width), BF16),
            pltpu.VMEM((levels, GROUP, bs, width), BF16),
            pltpu.VMEM((levels, GROUP, width, bs), BF16),
            pltpu.VMEM((levels, GROUP, width, bs), BF16),
            pltpu.VMEM((levels - 1, GROUP, width, bs), BF16),
            pltpu.VMEM((levels - 1, width, bs), BF16),
            pltpu.VMEM((levels - 1, REACH, width, bs), BF16),
            pltpu.VMEM((levels, GROUP, bs, width), BF16),
            dma((2,)), dma((parts, 2)), dma((2,)), dma((parts,)),
            dma((2, ncores - 1)), dma((2 * (levels + GROUP), ncores - 1)),
            dma, dma((levels,)), dma, dma,
            dma((2,)), dma((levels - 1, 2)), dma((2,)), dma((levels - 1, REACH)),
            dma, dma, dma, dma((2,)), dma, dma,
        ],
        compiler_params=pltpu.CompilerParams(
            collective_id=0, has_side_effects=True, vmem_limit_bytes=62 << 20
        ),
    )(neighbours, rhs, blocks, diag_inv)


def solution(mesh):
    placed = (
        P(None, "sweep", None, "cols"),
        P(None, "sweep", None, "cols", None),
        P(None, "sweep", "cols", None),
        P(None, "sweep", None),
    )
    return jax.shard_map(
        on_device,
        mesh=mesh,
        in_specs=placed,
        out_specs=P(None, "sweep", None, "cols"),
        check_vma=False,
    )
```

```python
import functools

import jax
import jax.numpy as jnp
from jax import lax
from jax.experimental import pallas as pl
from jax.experimental.pallas import tpu as pltpu
from jax.sharding import PartitionSpec as P

REACH = 5
GROUP = 4
F32 = jnp.float32
BF16 = jnp.bfloat16

SLOT = {0: 0, 4: 1, 1: 2, 2: 3, 3: 4, 5: 5}
DIAG = REACH + 1


def parts_of(levels):
    early = [(1, 2, 2), (1, 4, 2), (1, DIAG, 1)]
    for t in range(2, levels):
        early += [(t, 0, 4), (t, 4, 2), (t, DIAG, 1)]
    return early + [(1, 0, 2), (0, DIAG, 1)], len(early)


def mm(a, b):
    return jnp.dot(a, b, preferred_element_type=F32)


def mm_t(a, b):
    return lax.dot_general(a, b, (((1,), (1,)), ((), ())), preferred_element_type=F32)


def kernel(
    owners, ncores, neighbours, rhs, blocks, diag, out,
    nbr, fac, raw, wide, first, below, shifted, win, rloc, solved_t, samp_t, near, far, stage, ostage,
    s_own, r_own, s_dg, r_dg, s_core, r_core, s_rhs, r_rhs,
    s_up, r_up, s_x, r_x, s_b, r_b, r_half, s_o, r_o, s_raw, s_diag, s_wide, s_nbr,
):
    levels = rhs.shape[0]
    rows = diag.shape[2]
    slots = blocks.shape[2]
    width = rhs.shape[3] // GROUP
    planes = owners // GROUP
    top = levels - 1
    parts, n_early = parts_of(levels)
    me = lax.axis_index("sweep")
    c = lax.axis_index("cols")
    k = me // GROUP
    i = me % GROUP
    px = i + 1 - 2 * (i % 2)
    py = (i + 2) % GROUP
    dg = GROUP - 1 - i
    base = k * GROUP
    peers = (px, py, dg)
    sources = (i,) + peers
    cores = range(1, ncores)

    def at(owner, core):
        return (owner, core)

    def remote(src, dst, ssem, rsem, dev):
        return pltpu.make_async_remote_copy(
            src_ref=src, dst_ref=dst, send_sem=ssem, recv_sem=rsem,
            device_id=dev, device_id_type=pl.DeviceIdType.MESH,
        )

    barrier = pltpu.get_barrier_semaphore()

    def greet(owner, core):
        pl.semaphore_signal(
            barrier, inc=1, device_id=at(owner, core), device_id_type=pl.DeviceIdType.MESH
        )

    for q in peers:
        greet(base + q, c)
    for r in range(1, ncores):
        greet(me, (c + r) % ncores)
    count = 3 + ncores - 1
    for d in (1, 2):
        @pl.when(k >= d)
        def _():
            greet(me - d * GROUP, c)

        @pl.when(k + d < planes)
        def _():
            greet(me + d * GROUP, c)

        count = count + jnp.where(k >= d, 1, 0) + jnp.where(k + d < planes, 1, 0)

    mine = pl.ds(pl.multiple_of(c * rows, rows), rows)

    side = diag.shape[3] // 2
    for t in range(levels):
        for j in range(GROUP):
            fac[t, j, DIAG, 0:side, side:] = jnp.zeros((side, side), BF16)

    nbr_local = pltpu.make_async_copy(neighbours, nbr, s_nbr)
    raw_local = pltpu.make_async_copy(blocks.at[:, 0], raw, s_raw)
    diag_first = pltpu.make_async_copy(diag.at[0, 0], fac.at[0, i, DIAG, mine, :], s_diag.at[0])
    diag_rest = pltpu.make_async_copy(
        diag.at[1:, 0], fac.at[pl.ds(1, top), i, DIAG, mine, :], s_diag.at[1]
    )
    wide_local = pltpu.make_async_copy(rhs.at[0:2, 0], wide, s_wide)
    for local in (nbr_local, diag_first, raw_local, wide_local, diag_rest):
        local.start()

    def clear(ref):
        ref[...] = jnp.zeros_like(ref)

    @pl.when(k == 0)
    def _():
        clear(below)
        for l in range(levels - 1):
            clear(win.at[l, 0:REACH])

    @pl.when(k == 1)
    def _():
        for l in range(levels - 1):
            clear(win.at[l, 0])

    @pl.when(k + 1 >= planes)
    def _():
        clear(near)

    @pl.when((k + 1 >= planes) | (k < 1))
    def _():
        clear(far)

    def stage_level(t):
        for o in range(REACH + 1):
            slot, hit = jnp.int32(0), jnp.int32(0)
            for s in range(slots):
                got = nbr[t - 1, 0, s]
                same = (got == (t - 1) * owners + me - o) & (got >= 0)
                slot = jnp.where(same, s, slot)
                hit = jnp.where(same, 1, hit)
            block = raw[t - 1, slot].astype(F32) * hit.astype(F32)
            fac[t, i, SLOT[o], mine, :] = block.astype(BF16)

    half = rows // 2
    low = 2 * c < ncores

    def is_diag(p):
        return parts[p][1] == DIAG

    def each(p, is_low, act):
        if is_diag(p):
            pl.when(is_low)(lambda: act(side))
            pl.when(jnp.logical_not(is_low))(lambda: act(2 * side))
        else:
            act(2 * side)

    def shard(p, owner, wide_as, count=None):
        t, lo, n = parts[p]
        owner = owner if count is None else pl.ds(owner, count)
        return fac.at[t, owner, pl.ds(lo, n), mine, 0:wide_as]

    def shard_half(p, owner, h, wide_as):
        t, lo, n = parts[p]
        part = pl.ds(pl.multiple_of(c * rows + h * half, half), half)
        return fac.at[t, owner, pl.ds(lo, n), part, 0:wide_as]

    def settle(ref, sem):
        pltpu.make_async_copy(ref, ref, sem).wait()

    def core_spot(p, source):
        d = 1 if is_diag(p) else 0
        if p >= n_early:
            return 2 * (top - 1 + GROUP + d) + (1 if source else 0)
        t = parts[p][0]
        return 2 * (t - 1 if t < top else top - 1 + source) + d

    def own_copy(p, n, w):
        ref = shard(p, i, w)
        return remote(ref, ref, s_own.at[int(is_diag(p))], r_own.at[p, n], at(base + peers[n], c))

    def diag_copy(p, n, w):
        ref = shard_half(p, peers[n], n, w)
        return remote(ref, ref, s_dg.at[int(is_diag(p))], r_dg.at[p], at(base + peers[1 - n], c))

    def core_copy(p, source, r, w):
        ref = shard(p, sources[source], w)
        return remote(
            ref, ref, s_core.at[int(is_diag(p)), r - 1], r_core.at[core_spot(p, source), r - 1],
            at(me, (c + r) % ncores),
        )

    def columns(q):
        return pl.ds(pl.multiple_of(q * width, width), width)

    def deal(t, q):
        if t == 0:
            return first.at[:, columns(q)], win.at[0, REACH + i]
        if t == 1:
            return shifted.at[:, columns(q)], rloc.at[1, i]
        return rhs.at[t, 0, :, columns(q)], rloc.at[t, i]

    def deal_copy(t, n):
        src, dst = deal(t, peers[n])
        return remote(src, dst, s_rhs, r_rhs.at[t], at(base + peers[n], c))

    def deal_local(t):
        src, dst = deal(t, i)
        return pltpu.make_async_copy(src, dst, r_rhs.at[t])

    def deal_start(t):
        for n in range(3):
            deal_copy(t, n).start()
        deal_local(t).start()

    def deal_wait(t):
        settle(win.at[0, pl.ds(REACH, GROUP)] if t == 0 else rloc.at[t], r_rhs.at[t])

    def core_start(p, source):
        for r in cores:
            each(p, low, lambda w: core_copy(p, source, r, w).start())

    def core_wait(p, source, refs):
        for r in cores:
            is_low = 2 * ((c + ncores - r) % ncores) < ncores
            each(p, is_low, lambda w: settle(refs(w), r_core.at[core_spot(p, source), r - 1]))

    def core_wait_level(t, source, first_owner, count):
        p, lo = 3 * t - 3, 2 if t == 1 else 0
        owners_of = pl.ds(first_owner, count)
        core_wait(p, source, lambda w: fac.at[t, owners_of, pl.ds(lo, DIAG - lo), mine, :])

    def start(p):
        for n in range(2):
            each(p, low, lambda w: own_copy(p, n, w).start())

    def forward(p):
        for n in range(2):
            each(p, low, lambda w: own_copy(p, n, w).wait_recv())
            each(p, low, lambda w: diag_copy(p, n, w).start())
            core_start(p, 1 + n)

    def finish_diag(p):
        each(p, low, lambda w: settle(shard(p, i, w), r_dg.at[p]))
        core_start(p, 3)

    def up_copy():
        return remote(first, below, s_up, r_up, at(me + GROUP, c))

    def solved_copy(l, n):
        j = GROUP - 1 if n == GROUP else n
        step, spot = (2, 0) if n == GROUP else (1, 1 + n)
        return remote(
            win.at[l, REACH + j], win.at[l, spot], s_x.at[step - 1], r_x.at[l, step - 1],
            at(me + step * GROUP, c),
        )

    def solved_send(l, j):
        @pl.when(k + 1 < planes)
        def _():
            solved_copy(l, j).start()

        if j == GROUP - 1:
            @pl.when(k + 2 < planes)
            def _():
                solved_copy(l, GROUP).start()

    def solved_recv(l):
        @pl.when(k >= 1)
        def _():
            settle(win.at[l, pl.ds(1, GROUP)], r_x.at[l, 0])

        @pl.when(k >= 2)
        def _():
            settle(win.at[l, 0], r_x.at[l, 1])

    def residue(l, j):
        acc = None
        for o in range(REACH + 1):
            if l == 1 and SLOT[o] < 2:
                continue
            term = mm(fac[l, j, SLOT[o]], win[l - 1, REACH + j - o])
            acc = term if acc is None else acc + term
        return (rloc[l, j].astype(F32) - acc).astype(BF16)

    def solve_level(l):
        for j in reversed(range(GROUP)):
            y = mm(fac[l, j, DIAG], residue(l, j))
            win[l, REACH + j] = y.astype(BF16)
            solved_send(l, j)
            solved_t[l, j] = y.T.astype(BF16)

    late = (n_early, n_early + 1)
    nbr_local.wait()
    raw_local.wait()
    stage_level(1)
    diag_first.wait()
    diag_rest.wait()
    pl.semaphore_wait(barrier, count)

    core_start(late[1], 0)
    core_start(late[0], 0)
    start(0)
    for p in range(3):
        core_start(p, 0)
    wide_local.wait()
    core_wait(late[1], 0, lambda w: shard(late[1], i, w))
    first[...] = mm(fac[0, i, DIAG], wide[0]).astype(BF16)
    deal_start(0)

    @pl.when(k + 1 < planes)
    def _():
        up_copy().start()

    start(1)
    start(2)
    core_wait(late[0], 0, lambda w: shard(late[0], i, w))
    for t in range(2, levels):
        stage_level(t)
        for p in range(3 * t - 3, 3 * t):
            core_start(p, 0)
    forward(0)
    deal_wait(0)
    for j in reversed(range(GROUP)):
        solved_send(0, j)

    @pl.when(k >= 1)
    def _():
        up_copy().wait_recv()

    part = mm(fac[1, i, SLOT[0]], first[...]) + mm(fac[1, i, SLOT[4]], below[...])
    shifted[...] = (wide[1].astype(F32) - part).astype(BF16)
    deal_start(1)
    for j in range(GROUP):
        solved_t[0, j] = win[0, REACH + j].astype(F32).T.astype(BF16)
    forward(1)
    forward(2)
    for l in range(1, top):
        deal_start(l + 1)
        for p in range(3 * l, 3 * l + 3):
            start(p)
        for p in range(3 * l - 3, 3 * l):
            finish_diag(p)
        deal_wait(l)
        core_wait_level(l, 0, 0, GROUP)
        core_wait(3 * l - 1, 0, lambda w: shard(3 * l - 1, 0, w, GROUP))
        solved_recv(l - 1)
        solve_level(l)
        for p in range(3 * l, 3 * l + 3):
            forward(p)

    for p in late:
        start(p)
    deal_wait(top)
    solved_recv(top - 1)
    last = 3 * top - 1
    for source in range(GROUP):
        j = sources[source]
        if source == 3:
            for p in range(last - 2, last + 1):
                finish_diag(p)
        core_wait_level(top, source, 0, 1)
        res = residue(top, j).astype(F32).T.astype(BF16)
        core_wait(last, source, lambda w: shard(last, 0, w))
        adjusted = mm_t(res, fac[top, j, DIAG]).astype(BF16)
        samp_t[top, j] = mm(adjusted, fac[top, j, DIAG]).astype(BF16)

    def term_copy(l, n):
        dst = far.at[l] if n == 0 else near.at[l, n - 1]
        return remote(stage.at[l, n], dst, s_b.at[min(n, 1)], r_b.at[l, n], at(me - GROUP, c))

    halves = (pl.ds(side, side), pl.ds(0, side))

    def half_copy(h):
        return remote(
            stage.at[0, REACH - 1, :, halves[h]], near.at[0, GROUP - 1, :, halves[h]],
            s_b.at[1], r_half.at[h], at(me - GROUP, c),
        )

    def out_copy(l, q, part):
        return remote(
            ostage.at[l, q, part], out.at[l, 0, part, columns(i)], s_o, r_o, at(base + q, c)
        )

    def out_local(l, part):
        return pltpu.make_async_copy(
            ostage.at[l, i, part], out.at[l, 0, part, columns(i)], s_o
        )

    def emit_rows(l, j, part, turned):
        ostage[l, j, part] = turned.astype(F32).T.astype(BF16)

        @pl.when(i == j)
        def _():
            out_local(l, part).start()

        @pl.when(i != j)
        def _():
            out_copy(l, j, part).start()

    def emit(l, j):
        emit_rows(l, j, pl.ds(0, 2 * side), samp_t[l, j])

    def terms(l, w):
        total = None
        for j in range(max(0, w - REACH), min(GROUP - 1, w) + 1):
            term = mm(samp_t[l + 1, j], fac[l + 1, j, SLOT[REACH + j - w]])
            total = term if total is None else total + term
        return total

    def ship(l, w):
        total = terms(l, w)
        if w == REACH - 1:
            @pl.when((k + 1 < planes) & (k >= 1))
            def _():
                term_copy(l, 0).wait_recv()

            total = total + far[l].astype(F32)
        stage[l, w] = total.astype(BF16)

        @pl.when(k >= (2 if w == 0 else 1))
        def _():
            if l == 0 and w == REACH - 1:
                for h in range(2):
                    half_copy(h).start()
            else:
                term_copy(l, w).start()

    for w in range(REACH):
        ship(top - 1, w)
    for l in range(top - 1, -1, -1):
        for j in range(GROUP):
            emit(l + 1, j)
        back = [terms(l, REACH + j) for j in range(GROUP)]
        for j in range(GROUP if l > 0 else GROUP - 1):
            @pl.when(k + 1 < planes)
            def _():
                term_copy(l, j + 1).wait_recv()

            total = back[j] + near[l, j].astype(F32)
            adjusted = (solved_t[l, j].astype(F32) - total).astype(BF16)
            samp_t[l, j] = mm(adjusted, fac[l, j, DIAG]).astype(BF16)
            if l > 0:
                for w in range(REACH):
                    if min(GROUP - 1, w) == j:
                        ship(l - 1, w)
            else:
                emit(l, j)
            if l == top - 1 and j == 1:
                for p in late:
                    forward(p)
        if l == top - 1:
            for p in late:
                finish_diag(p)
            for p in late:
                core_wait(p, 1, lambda w: shard(p, 0, w, GROUP - 1))

    j = GROUP - 1
    upper = None
    for h in range(2):
        cut = slice(side, 2 * side) if h == 0 else slice(0, side)

        @pl.when(k + 1 < planes)
        def _():
            half_copy(h).wait_recv()

        total = back[j][:, cut] + near[0, j, :, cut].astype(F32)
        adjusted = (solved_t[0, j, :, cut].astype(F32) - total).astype(BF16)
        sample = mm(adjusted, fac[0, j, DIAG, cut, cut])
        if h == 0:
            upper = mm(adjusted, fac[0, j, DIAG, side:, 0:side])
        else:
            sample = sample + upper
        emit_rows(0, j, halves[h], sample.astype(BF16))

    def sent(spot, levels_of, slots_of, w):
        settle(fac.at[levels_of, 0:2, slots_of, mine, 0:w], s_own.at[spot])
        settle(fac.at[levels_of, 0:1, slots_of, mine, 0:w], s_dg.at[spot])
        for r in cores:
            settle(fac.at[levels_of, 0:GROUP, slots_of, mine, 0:w], s_core.at[spot, r - 1])

    sent(0, pl.ds(1, top), pl.ds(0, DIAG), 2 * side)
    each(late[1], low, lambda w: sent(1, pl.ds(0, levels), pl.ds(DIAG, 1), w))
    settle(rloc.at[:, pl.ds(0, 3)], s_rhs)

    @pl.when(k + 1 < planes)
    def _():
        settle(first, s_up)
        settle(win.at[:, pl.ds(0, GROUP)], s_x.at[0])

    @pl.when(k + 2 < planes)
    def _():
        settle(win.at[:, 0], s_x.at[1])

    @pl.when(k >= 1)
    def _():
        settle(stage.at[:, pl.ds(1, REACH - 1)], s_b.at[1])

    @pl.when(k >= 2)
    def _():
        settle(stage.at[:, 0], s_b.at[0])

    settle(ostage, s_o)
    settle(ostage.at[:, pl.ds(0, 3)], r_o)


def on_device(rhs, blocks, diag_inv, neighbours):
    owners = lax.axis_size("sweep")
    ncores = lax.axis_size("cols")
    levels, _, bs, cols = rhs.shape
    width = cols // GROUP
    parts = len(parts_of(levels)[0])
    dma = pltpu.SemaphoreType.DMA
    hbm = pl.BlockSpec(memory_space=pltpu.HBM)
    return pl.pallas_call(
        functools.partial(kernel, owners, ncores),
        out_shape=pltpu.VMEM(rhs.shape, rhs.dtype),
        in_specs=[hbm, hbm, hbm, hbm],
        out_specs=pl.BlockSpec(memory_space=pltpu.VMEM),
        scratch_shapes=[
            pltpu.SMEM(neighbours.shape, jnp.int32),
            pltpu.VMEM((levels, GROUP, REACH + 2, bs, bs), BF16),
            pltpu.VMEM(blocks.shape[:1] + blocks.shape[2:], BF16),
            pltpu.VMEM((2, bs, cols), BF16),
            pltpu.VMEM((bs, cols), BF16),
            pltpu.VMEM((bs, cols), BF16),
            pltpu.VMEM((bs, cols), BF16),
            pltpu.VMEM((levels - 1, REACH + GROUP, bs, width), BF16),
            pltpu.VMEM((levels, GROUP, bs, width), BF16),
            pltpu.VMEM((levels, GROUP, width, bs), BF16),
            pltpu.VMEM((levels, GROUP, width, bs), BF16),
            pltpu.VMEM((levels - 1, GROUP, width, bs), BF16),
            pltpu.VMEM((levels - 1, width, bs), BF16),
            pltpu.VMEM((levels - 1, REACH, width, bs), BF16),
            pltpu.VMEM((levels, GROUP, bs, width), BF16),
            dma((2,)), dma((parts, 2)), dma((2,)), dma((parts,)),
            dma((2, ncores - 1)), dma((2 * (levels + GROUP), ncores - 1)),
            dma, dma((levels,)), dma, dma,
            dma((2,)), dma((levels - 1, 2)), dma((2,)), dma((levels - 1, REACH)), dma((2,)),
            dma, dma, dma, dma((2,)), dma, dma,
        ],
        compiler_params=pltpu.CompilerParams(
            collective_id=0, has_side_effects=True, vmem_limit_bytes=62 << 20
        ),
    )(neighbours, rhs, blocks, diag_inv)


def solution(mesh):
    placed = (
        P(None, "sweep", None, "cols"),
        P(None, "sweep", None, "cols", None),
        P(None, "sweep", "cols", None),
        P(None, "sweep", None),
    )
    return jax.shard_map(
        on_device,
        mesh=mesh,
        in_specs=placed,
        out_specs=P(None, "sweep", None, "cols"),
        check_vma=False,
    )
```

```python
import functools

import jax
import jax.numpy as jnp
from jax import lax
from jax.experimental import pallas as pl
from jax.experimental.pallas import tpu as pltpu
from jax.sharding import PartitionSpec as P

REACH = 5
GROUP = 4
F32 = jnp.float32
BF16 = jnp.bfloat16

SLOT = {0: 0, 4: 1, 1: 2, 2: 3, 3: 4, 5: 5}
DIAG = REACH + 1


def parts_of(levels):
    early = [(1, 2, 2), (1, 4, 2), (1, DIAG, 1)]
    for t in range(2, levels):
        early += [(t, 0, 4), (t, 4, 2), (t, DIAG, 1)]
    return early + [(1, 0, 2), (0, DIAG, 1)], len(early)


def mm(a, b):
    return jnp.dot(a, b, preferred_element_type=F32)


def mm_t(a, b):
    return lax.dot_general(a, b, (((1,), (1,)), ((), ())), preferred_element_type=F32)


def kernel(
    owners, ncores, neighbours, rhs, blocks, diag, out,
    nbr, fac, raw, wide, first, below, shifted, passing, crossed, win, rloc, solved_t, samp_t, near, far, stage, ostage,
    s_own, r_own, s_dg, r_dg, s_core, r_core, s_rhs, r_rhs,
    s_up, r_up, s_x, r_x, s_b, r_b, r_half, s_o, r_o, s_raw, s_diag, s_wide, s_nbr, s_pass, r_pass,
):
    levels = rhs.shape[0]
    rows = diag.shape[2]
    slots = blocks.shape[2]
    width = rhs.shape[3] // GROUP
    planes = owners // GROUP
    top = levels - 1
    parts, n_early = parts_of(levels)
    me = lax.axis_index("sweep")
    c = lax.axis_index("cols")
    k = me // GROUP
    i = me % GROUP
    px = i + 1 - 2 * (i % 2)
    py = (i + 2) % GROUP
    dg = GROUP - 1 - i
    base = k * GROUP
    peers = (px, py, dg)
    sources = (i,) + peers
    cores = range(1, ncores)

    def at(owner, core):
        return (owner, core)

    def remote(src, dst, ssem, rsem, dev):
        return pltpu.make_async_remote_copy(
            src_ref=src, dst_ref=dst, send_sem=ssem, recv_sem=rsem,
            device_id=dev, device_id_type=pl.DeviceIdType.MESH,
        )

    barrier = pltpu.get_barrier_semaphore()

    def greet(owner, core):
        pl.semaphore_signal(
            barrier, inc=1, device_id=at(owner, core), device_id_type=pl.DeviceIdType.MESH
        )

    for q in peers:
        greet(base + q, c)
    for r in range(1, ncores):
        greet(me, (c + r) % ncores)
    count = 3 + ncores - 1
    detour = planes == 4
    for d in (1, 2, 3) if detour else (1, 2):
        @pl.when(k >= d)
        def _():
            greet(me - d * GROUP, c)

        @pl.when(k + d < planes)
        def _():
            greet(me + d * GROUP, c)

        count = count + jnp.where(k >= d, 1, 0) + jnp.where(k + d < planes, 1, 0)

    mine = pl.ds(pl.multiple_of(c * rows, rows), rows)

    side = diag.shape[3] // 2
    for t in range(levels):
        for j in range(GROUP):
            fac[t, j, DIAG, 0:side, side:] = jnp.zeros((side, side), BF16)

    nbr_local = pltpu.make_async_copy(neighbours, nbr, s_nbr)
    raw_local = pltpu.make_async_copy(blocks.at[:, 0], raw, s_raw)
    diag_first = pltpu.make_async_copy(diag.at[0, 0], fac.at[0, i, DIAG, mine, :], s_diag.at[0])
    diag_rest = pltpu.make_async_copy(
        diag.at[1:, 0], fac.at[pl.ds(1, top), i, DIAG, mine, :], s_diag.at[1]
    )
    wide_local = pltpu.make_async_copy(rhs.at[0:2, 0], wide, s_wide)
    for local in (nbr_local, diag_first, raw_local, wide_local, diag_rest):
        local.start()

    def clear(ref):
        ref[...] = jnp.zeros_like(ref)

    @pl.when(k == 0)
    def _():
        for t in range(1, levels):
            for j in range(GROUP):
                clear(fac.at[t, j, SLOT[REACH]])
        clear(below)
        for l in range(levels - 1):
            clear(win.at[l, 0:REACH])

    @pl.when(k == 1)
    def _():
        for l in range(levels - 1):
            clear(win.at[l, 0])

    @pl.when(k + 1 >= planes)
    def _():
        clear(near)

    @pl.when((k + 1 >= planes) | (k < 1))
    def _():
        clear(far)

    def stage_level(t):
        for o in range(REACH + 1):
            slot, hit = jnp.int32(0), jnp.int32(0)
            for s in range(slots):
                got = nbr[t - 1, 0, s]
                same = (got == (t - 1) * owners + me - o) & (got >= 0)
                slot = jnp.where(same, s, slot)
                hit = jnp.where(same, 1, hit)
            block = raw[t - 1, slot].astype(F32) * hit.astype(F32)
            fac[t, i, SLOT[o], mine, :] = block.astype(BF16)

    half = rows // 2
    low = 2 * c < ncores

    def is_diag(p):
        return parts[p][1] == DIAG

    def each(p, is_low, act):
        _, lo, n = parts[p]
        if is_diag(p):
            pl.when(is_low)(lambda: act((side, n)))
            pl.when(jnp.logical_not(is_low))(lambda: act((2 * side, n)))
        elif lo + n == DIAG:
            pl.when(k == 0)(lambda: act((2 * side, n - 1)))
            pl.when(k > 0)(lambda: act((2 * side, n)))
        else:
            act((2 * side, n))

    def shard(p, owner, wide_as, count=None):
        t, lo, _ = parts[p]
        owner = owner if count is None else pl.ds(owner, count)
        return fac.at[t, owner, pl.ds(lo, wide_as[1]), mine, 0:wide_as[0]]

    def shard_half(p, owner, h, wide_as):
        t, lo, _ = parts[p]
        part = pl.ds(pl.multiple_of(c * rows + h * half, half), half)
        return fac.at[t, owner, pl.ds(lo, wide_as[1]), part, 0:wide_as[0]]

    def settle(ref, sem):
        pltpu.make_async_copy(ref, ref, sem).wait()

    def core_spot(p, source):
        d = 1 if is_diag(p) else 0
        if p >= n_early:
            return 2 * (top - 1 + GROUP + d) + (1 if source else 0)
        t = parts[p][0]
        return 2 * (t - 1 if t < top else top - 1 + source) + d

    def own_copy(p, n, w):
        ref = shard(p, i, w)
        return remote(ref, ref, s_own.at[int(is_diag(p))], r_own.at[p, n], at(base + peers[n], c))

    def diag_copy(p, n, w):
        ref = shard_half(p, peers[n], n, w)
        return remote(ref, ref, s_dg.at[int(is_diag(p))], r_dg.at[p], at(base + peers[1 - n], c))

    def core_copy(p, source, r, w):
        ref = shard(p, sources[source], w)
        return remote(
            ref, ref, s_core.at[int(is_diag(p)), r - 1], r_core.at[core_spot(p, source), r - 1],
            at(me, (c + r) % ncores),
        )

    def columns(q):
        return pl.ds(pl.multiple_of(q * width, width), width)

    def deal(t, q):
        if t == 0:
            return first.at[:, columns(q)], win.at[0, REACH + i]
        if t == 1:
            return shifted.at[:, columns(q)], rloc.at[1, i]
        return rhs.at[t, 0, :, columns(q)], rloc.at[t, i]

    def deal_copy(t, n):
        src, dst = deal(t, peers[n])
        return remote(src, dst, s_rhs, r_rhs.at[t], at(base + peers[n], c))

    def deal_local(t):
        src, dst = deal(t, i)
        return pltpu.make_async_copy(src, dst, r_rhs.at[t])

    def pass_down(z):
        return remote(
            rhs.at[top, 0, :, columns(dg)], passing.at[z], s_rhs, r_pass.at[0],
            at(me - (z + 1) * GROUP, c),
        )

    def pass_across(z):
        return remote(
            passing.at[z], crossed.at[z], s_pass.at[0], r_pass.at[1], at(base + dg, c)
        )

    def pass_up(z):
        return remote(
            crossed.at[z], rloc.at[top, dg], s_pass.at[1], r_rhs.at[top],
            at(me + (z + 1) * GROUP, c),
        )

    def pass_on(step):
        for z in range(3 if detour else 0):
            if step == 0:
                pl.when(k == z + 1)(lambda: pass_down(z).start())
            else:
                @pl.when(k == 0)
                def _():
                    if z == 0:
                        settle(passing, r_pass.at[step - 1])
                    (pass_across if step == 1 else pass_up)(z).start()

    def deal_start(t):
        for n in range(3):
            if detour and t == top and n == 2:
                pl.when(k == 0)(lambda: deal_copy(t, n).start())
            else:
                deal_copy(t, n).start()
        deal_local(t).start()

    def deal_wait(t):
        settle(win.at[0, pl.ds(REACH, GROUP)] if t == 0 else rloc.at[t], r_rhs.at[t])

    def core_start(p, source):
        for r in cores:
            each(p, low, lambda w: core_copy(p, source, r, w).start())

    def core_wait(p, source, refs):
        for r in cores:
            is_low = 2 * ((c + ncores - r) % ncores) < ncores
            each(p, is_low, lambda w: settle(refs(w), r_core.at[core_spot(p, source), r - 1]))

    def core_wait_level(t, source, first_owner, count):
        p, lo = 3 * t - 3, 2 if t == 1 else 0
        owners_of = pl.ds(first_owner, count)
        for cond, end in ((k == 0, DIAG - 1), (k > 0, DIAG)):
            pl.when(cond)(
                lambda: core_wait(
                    p, source, lambda w: fac.at[t, owners_of, pl.ds(lo, end - lo), mine, :]
                )
            )

    def start(p):
        for n in range(2):
            each(p, low, lambda w: own_copy(p, n, w).start())

    def forward(p):
        for n in range(2):
            each(p, low, lambda w: own_copy(p, n, w).wait_recv())
            each(p, low, lambda w: diag_copy(p, n, w).start())
            core_start(p, 1 + n)

    def finish_diag(p):
        each(p, low, lambda w: settle(shard(p, i, w), r_dg.at[p]))
        core_start(p, 3)

    def up_copy():
        return remote(first, below, s_up, r_up, at(me + GROUP, c))

    def solved_copy(l, n):
        j = GROUP - 1 if n == GROUP else n
        step, spot = (2, 0) if n == GROUP else (1, 1 + n)
        return remote(
            win.at[l, REACH + j], win.at[l, spot], s_x.at[step - 1], r_x.at[l, step - 1],
            at(me + step * GROUP, c),
        )

    def solved_send(l, j):
        @pl.when(k + 1 < planes)
        def _():
            solved_copy(l, j).start()

        if j == GROUP - 1:
            @pl.when(k + 2 < planes)
            def _():
                solved_copy(l, GROUP).start()

    def solved_recv(l):
        @pl.when(k >= 1)
        def _():
            settle(win.at[l, pl.ds(1, GROUP)], r_x.at[l, 0])

        @pl.when(k >= 2)
        def _():
            settle(win.at[l, 0], r_x.at[l, 1])

    def residue(l, j):
        acc = None
        for o in range(REACH + 1):
            if l == 1 and SLOT[o] < 2:
                continue
            term = mm(fac[l, j, SLOT[o]], win[l - 1, REACH + j - o])
            acc = term if acc is None else acc + term
        return (rloc[l, j].astype(F32) - acc).astype(BF16)

    def solve_level(l):
        for j in reversed(range(GROUP)):
            y = mm(fac[l, j, DIAG], residue(l, j))
            win[l, REACH + j] = y.astype(BF16)
            solved_send(l, j)
            solved_t[l, j] = y.T.astype(BF16)

    late = (n_early, n_early + 1)
    nbr_local.wait()
    raw_local.wait()
    stage_level(1)
    diag_first.wait()
    diag_rest.wait()
    pl.semaphore_wait(barrier, count)

    core_start(late[1], 0)
    core_start(late[0], 0)
    start(0)
    for p in range(3):
        core_start(p, 0)
    wide_local.wait()
    core_wait(late[1], 0, lambda w: shard(late[1], i, w))
    first[...] = mm(fac[0, i, DIAG], wide[0]).astype(BF16)
    deal_start(0)

    @pl.when(k + 1 < planes)
    def _():
        up_copy().start()

    pass_on(0)
    start(1)
    start(2)
    core_wait(late[0], 0, lambda w: shard(late[0], i, w))
    for t in range(2, levels):
        stage_level(t)
        for p in range(3 * t - 3, 3 * t):
            core_start(p, 0)
    forward(0)
    deal_wait(0)
    for j in reversed(range(GROUP)):
        solved_send(0, j)

    @pl.when(k >= 1)
    def _():
        up_copy().wait_recv()

    part = mm(fac[1, i, SLOT[0]], first[...]) + mm(fac[1, i, SLOT[4]], below[...])
    shifted[...] = (wide[1].astype(F32) - part).astype(BF16)
    deal_start(1)
    for j in range(GROUP):
        solved_t[0, j] = win[0, REACH + j].astype(F32).T.astype(BF16)
    forward(1)
    pass_on(1)
    forward(2)
    for l in range(1, top):
        deal_start(l + 1)
        for p in range(3 * l, 3 * l + 3):
            start(p)
        for p in range(3 * l - 3, 3 * l):
            finish_diag(p)
        deal_wait(l)
        core_wait_level(l, 0, 0, GROUP)
        core_wait(3 * l - 1, 0, lambda w: shard(3 * l - 1, 0, w, GROUP))
        solved_recv(l - 1)
        if l == 1:
            pass_on(2)
        solve_level(l)
        for p in range(3 * l, 3 * l + 3):
            forward(p)

    for p in late:
        start(p)
    deal_wait(top)
    solved_recv(top - 1)
    last = 3 * top - 1
    for source in range(GROUP):
        j = sources[source]
        if source == 3:
            for p in range(last - 2, last + 1):
                finish_diag(p)
        core_wait_level(top, source, 0, 1)
        res = residue(top, j).astype(F32).T.astype(BF16)
        core_wait(last, source, lambda w: shard(last, 0, w))
        adjusted = mm_t(res, fac[top, j, DIAG]).astype(BF16)
        samp_t[top, j] = mm(adjusted, fac[top, j, DIAG]).astype(BF16)

    def term_copy(l, n):
        dst = far.at[l] if n == 0 else near.at[l, n - 1]
        return remote(stage.at[l, n], dst, s_b.at[min(n, 1)], r_b.at[l, n], at(me - GROUP, c))

    halves = (pl.ds(side, side), pl.ds(0, side))

    def half_copy(h):
        return remote(
            stage.at[0, REACH - 1, :, halves[h]], near.at[0, GROUP - 1, :, halves[h]],
            s_b.at[1], r_half.at[h], at(me - GROUP, c),
        )

    def out_copy(l, q, part):
        return remote(
            ostage.at[l, q, part], out.at[l, 0, part, columns(i)], s_o, r_o, at(base + q, c)
        )

    def out_local(l, part):
        return pltpu.make_async_copy(
            ostage.at[l, i, part], out.at[l, 0, part, columns(i)], s_o
        )

    def emit_rows(l, j, part, turned):
        ostage[l, j, part] = turned.astype(F32).T.astype(BF16)

        @pl.when(i == j)
        def _():
            out_local(l, part).start()

        @pl.when(i != j)
        def _():
            out_copy(l, j, part).start()

    def emit(l, j):
        emit_rows(l, j, pl.ds(0, 2 * side), samp_t[l, j])

    def terms(l, w):
        total = None
        for j in range(max(0, w - REACH), min(GROUP - 1, w) + 1):
            term = mm(samp_t[l + 1, j], fac[l + 1, j, SLOT[REACH + j - w]])
            total = term if total is None else total + term
        return total

    def ship(l, w):
        total = terms(l, w)
        if w == REACH - 1:
            @pl.when((k + 1 < planes) & (k >= 1))
            def _():
                term_copy(l, 0).wait_recv()

            total = total + far[l].astype(F32)
        stage[l, w] = total.astype(BF16)

        @pl.when(k >= (2 if w == 0 else 1))
        def _():
            if l == 0 and w == REACH - 1:
                for h in range(2):
                    half_copy(h).start()
            else:
                term_copy(l, w).start()

    for w in range(REACH):
        ship(top - 1, w)
    for l in range(top - 1, -1, -1):
        for j in range(GROUP):
            emit(l + 1, j)
        back = [terms(l, REACH + j) for j in range(GROUP)]
        for j in range(GROUP if l > 0 else GROUP - 1):
            @pl.when(k + 1 < planes)
            def _():
                term_copy(l, j + 1).wait_recv()

            total = back[j] + near[l, j].astype(F32)
            adjusted = (solved_t[l, j].astype(F32) - total).astype(BF16)
            samp_t[l, j] = mm(adjusted, fac[l, j, DIAG]).astype(BF16)
            if l > 0:
                for w in range(REACH):
                    if min(GROUP - 1, w) == j:
                        ship(l - 1, w)
            else:
                emit(l, j)
            if l == top - 1 and j == 1:
                for p in late:
                    forward(p)
        if l == top - 1:
            for p in late:
                finish_diag(p)
            for p in late:
                core_wait(p, 1, lambda w: shard(p, 0, w, GROUP - 1))

    j = GROUP - 1
    upper = None
    for h in range(2):
        cut = slice(side, 2 * side) if h == 0 else slice(0, side)

        @pl.when(k + 1 < planes)
        def _():
            half_copy(h).wait_recv()

        total = back[j][:, cut] + near[0, j, :, cut].astype(F32)
        adjusted = (solved_t[0, j, :, cut].astype(F32) - total).astype(BF16)
        sample = mm(adjusted, fac[0, j, DIAG, cut, cut])
        if h == 0:
            upper = mm(adjusted, fac[0, j, DIAG, side:, 0:side])
        else:
            sample = sample + upper
        emit_rows(0, j, halves[h], sample.astype(BF16))

    def sent(spot, levels_of, slots_of, w):
        settle(fac.at[levels_of, 0:2, slots_of, mine, 0:w], s_own.at[spot])
        settle(fac.at[levels_of, 0:1, slots_of, mine, 0:w], s_dg.at[spot])
        for r in cores:
            settle(fac.at[levels_of, 0:GROUP, slots_of, mine, 0:w], s_core.at[spot, r - 1])

    pl.when(k == 0)(lambda: sent(0, pl.ds(1, top), pl.ds(0, DIAG - 1), 2 * side))
    pl.when(k > 0)(lambda: sent(0, pl.ds(1, top), pl.ds(0, DIAG), 2 * side))
    each(late[1], low, lambda w: sent(1, pl.ds(0, levels), pl.ds(DIAG, 1), w[0]))
    settle(rloc.at[:, pl.ds(0, 3)], s_rhs)
    if detour:
        @pl.when(k == 0)
        def _():
            for step in range(2):
                settle(passing, s_pass.at[step])

    @pl.when(k + 1 < planes)
    def _():
        settle(first, s_up)
        settle(win.at[:, pl.ds(0, GROUP)], s_x.at[0])

    @pl.when(k + 2 < planes)
    def _():
        settle(win.at[:, 0], s_x.at[1])

    @pl.when(k >= 1)
    def _():
        settle(stage.at[:, pl.ds(1, REACH - 1)], s_b.at[1])

    @pl.when(k >= 2)
    def _():
        settle(stage.at[:, 0], s_b.at[0])

    settle(ostage, s_o)
    settle(ostage.at[:, pl.ds(0, 3)], r_o)


def on_device(rhs, blocks, diag_inv, neighbours):
    owners = lax.axis_size("sweep")
    ncores = lax.axis_size("cols")
    levels, _, bs, cols = rhs.shape
    width = cols // GROUP
    parts = len(parts_of(levels)[0])
    dma = pltpu.SemaphoreType.DMA
    hbm = pl.BlockSpec(memory_space=pltpu.HBM)
    return pl.pallas_call(
        functools.partial(kernel, owners, ncores),
        out_shape=pltpu.VMEM(rhs.shape, rhs.dtype),
        in_specs=[hbm, hbm, hbm, hbm],
        out_specs=pl.BlockSpec(memory_space=pltpu.VMEM),
        scratch_shapes=[
            pltpu.SMEM(neighbours.shape, jnp.int32),
            pltpu.VMEM((levels, GROUP, REACH + 2, bs, bs), BF16),
            pltpu.VMEM(blocks.shape[:1] + blocks.shape[2:], BF16),
            pltpu.VMEM((2, bs, cols), BF16),
            pltpu.VMEM((bs, cols), BF16),
            pltpu.VMEM((bs, cols), BF16),
            pltpu.VMEM((bs, cols), BF16),
            pltpu.VMEM((3, bs, width), BF16),
            pltpu.VMEM((3, bs, width), BF16),
            pltpu.VMEM((levels - 1, REACH + GROUP, bs, width), BF16),
            pltpu.VMEM((levels, GROUP, bs, width), BF16),
            pltpu.VMEM((levels, GROUP, width, bs), BF16),
            pltpu.VMEM((levels, GROUP, width, bs), BF16),
            pltpu.VMEM((levels - 1, GROUP, width, bs), BF16),
            pltpu.VMEM((levels - 1, width, bs), BF16),
            pltpu.VMEM((levels - 1, REACH, width, bs), BF16),
            pltpu.VMEM((levels, GROUP, bs, width), BF16),
            dma((2,)), dma((parts, 2)), dma((2,)), dma((parts,)),
            dma((2, ncores - 1)), dma((2 * (levels + GROUP), ncores - 1)),
            dma, dma((levels,)), dma, dma,
            dma((2,)), dma((levels - 1, 2)), dma((2,)), dma((levels - 1, REACH)), dma((2,)),
            dma, dma, dma, dma((2,)), dma, dma, dma((2,)), dma((2,)),
        ],
        compiler_params=pltpu.CompilerParams(
            collective_id=0, has_side_effects=True, vmem_limit_bytes=62 << 20
        ),
    )(neighbours, rhs, blocks, diag_inv)


def solution(mesh):
    placed = (
        P(None, "sweep", None, "cols"),
        P(None, "sweep", None, "cols", None),
        P(None, "sweep", "cols", None),
        P(None, "sweep", None),
    )
    return jax.shard_map(
        on_device,
        mesh=mesh,
        in_specs=placed,
        out_specs=P(None, "sweep", None, "cols"),
        check_vma=False,
    )
```
